32 devices in a mesh: sub: 4 (over z), row: 2 (over core), col: 4 (over y, x).
Axes of the slice: x: 2, y: 2, z: 4, core: 2. Of those that a mesh axis runs over, the one named last changes fastest.
Arguments:
- factor_cols: bfloat16 [4, 2, 2048, 4096], P('sub', None, 'col', 'row'), may hold values from -0.09375 to 0.09375
- block_pattern: int32 [4, 16, 16], P('sub'), may hold values 0 or 1
- diag_inverse: float32 [4, 4096, 2048], P('sub', ('row', 'col')), may hold values from -1 to 2
- coupling_cols: bfloat16 [4, 2, 2048, 1024], P('sub', 'row', 'col'), may hold values from -0.09375 to 0.09375
- separator_rows: int32 [4, 1024], P('sub'), may hold values from 0 to 1535, as said below
- root_inverse: float32 [1536, 1536], P('col'), may hold values from -1 to 2
- right_side: float32 [4, 4096, 128], P('sub', 'row'), may hold values from -6 to 6
- root_right: float32 [1536, 128], P('col'), may hold values from -6 to 6
Outputs:
- solution: float32 [4, 4096, 128], P('sub', ('row', 'col'))
- root_solution: float32 [1536, 128], P('col')
The draws below stay inside these ranges and needn't reach their ends.
Inputs may be any that keep to these rules, and one draw needn't show every extreme that they name: `separator_rows`: within one section the 1024 entries are distinct.
All inputs are finite; a program needn't handle non-finite values. No bound on the sum of `block_pattern` on one device may be relied on, other than what follows from the above.
Results may differ from the reference program's by a relative error of at most 0.003.
Values may be sent and summed in bfloat16 or wider, within the bound.
A program may use at most 64 MiB of HBM per device.

```python
import jax
import jax.numpy as jnp
from jax import lax

BLOCK = 256
SOURCES = 128
SEPARATOR = 1536
COUPLED = 1024
PANEL = 2048
PANELS = 2
SECTION = 4096
BLOCKS = 16
SECTIONS = 4


def inverse_blocks(key, count, order):
    noise = jnp.clip(jax.random.normal(key, (count, order, order), jnp.float32), -6.0, 6.0)
    return jnp.eye(order, dtype=jnp.float32)[None] + 0.3 * noise / jnp.sqrt(order * 1.0)


def draw_diag_inverse(key, part):
    blocks = inverse_blocks(jax.random.fold_in(key, 11), SECTIONS * PANELS, PANEL)
    return blocks.reshape(SECTIONS, SECTION, PANEL)


def draw_root_inverse(key, part):
    return inverse_blocks(jax.random.fold_in(key, 13), 1, SEPARATOR)[0]


def draw_separator_rows(key, part):

    def one_section(section_key):
        first_key, second_key = jax.random.split(section_key)
        inner = jax.random.permutation(first_key, SEPARATOR - 2)[:COUPLED - 2] + 1
        values = jnp.concatenate([jnp.array([0, SEPARATOR - 1], jnp.int32), inner.astype(jnp.int32)])
        return values[jax.random.permutation(second_key, COUPLED)]
    return jax.vmap(one_section)(jax.random.split(jax.random.fold_in(key, 17), SECTIONS))


def place_ends(values, stream_key, low, top_value):
    place = [jax.random.randint(jax.random.fold_in(stream_key, axis), (), 0, length) for axis, length in enumerate(values.shape)]
    widest = values.shape.index(max(values.shape))
    beside = place[:widest] + [(place[widest] + 1) % values.shape[widest]] + place[widest + 1:]
    return values.at[tuple(place)].set(low).at[tuple(beside)].set(top_value)


def steps_of(own_key, extent, cuts, smallest, high):
    loudness = 1.0
    for axis_at, shards_of in cuts:
        heights = jax.random.uniform(jax.random.fold_in(jax.random.fold_in(own_key, 6), axis_at), (shards_of,), jnp.float32, smallest / len(cuts), high / len(cuts))
        loudness = loudness * jnp.repeat(jnp.exp(heights), extent[axis_at] // shards_of).reshape((-1,) + (1,) * (len(extent) - 1 - axis_at))
    return loudness


def normal_values(key, dims, width, most, shards=(), kind=jnp.bfloat16):
    entries = jax.random.normal(key, dims, jnp.float32) * width
    if len(shards) > 0:
        entries = steps_of(key, dims, shards, -0.22, 0.18) * entries
    return jnp.clip(entries, min=-most, max=most).astype(kind)


def setup_inputs(seed: int = 0) -> dict:
    seeds = jax.random.split(jax.random.key(seed), 9)
    factor_cols = normal_values(seeds[0], (SECTIONS, PANELS, PANEL, SECTION), SECTION ** -0.5, 0.09375, ((0, 4), (2, 4), (3, 2)))
    block_pattern = place_ends((jax.random.randint(seeds[1], (SECTIONS, BLOCKS, BLOCKS), 0, 3) < 2).astype(jnp.int32), jax.random.fold_in(seeds[1], 1), 0, 1)
    diag_inverse = draw_diag_inverse(jax.random.fold_in(seeds[8], 71), 0)
    coupling_cols = normal_values(seeds[3], (SECTIONS, PANELS, PANEL, COUPLED), SECTION ** -0.5, 0.09375, ((0, 4), (1, 2), (2, 4)))
    separator_rows = draw_separator_rows(jax.random.fold_in(seeds[8], 71), 0)
    root_inverse = draw_root_inverse(jax.random.fold_in(seeds[8], 71), 0)
    right_side = normal_values(seeds[6], (SECTIONS, SECTION, SOURCES), 1.0, 6.0, ((0, 4), (1, 2)), jnp.float32)
    root_right = normal_values(seeds[7], (SEPARATOR, SOURCES), 1.0, 6.0, ((0, 4),), jnp.float32)
    return {"factor_cols": factor_cols, "block_pattern": block_pattern, "diag_inverse": diag_inverse, "coupling_cols": coupling_cols, "separator_rows": separator_rows, "root_inverse": root_inverse, "right_side": right_side, "root_right": root_right}


precise = lax.Precision.HIGHEST


def reference(factor_cols, block_pattern, diag_inverse, coupling_cols, separator_rows, root_inverse, right_side, root_right):
    positions = jnp.arange(SECTION)
    row_panels = positions // PANEL
    below_all = row_panels[:, None] > row_panels[None, :]
    separator_ids = jnp.arange(SEPARATOR)
    mapped_total = jnp.zeros((SEPARATOR, SOURCES), jnp.float32)
    kept = []
    for section in range(SECTIONS):
        expanded = jnp.repeat(jnp.repeat(block_pattern[section], BLOCK, axis=0), BLOCK, axis=1)
        lower_mask = jnp.where(below_all, expanded, 0).astype(jnp.bfloat16)
        masked_cols = factor_cols[section].reshape(SECTION, SECTION) * lower_mask.T
        coupled = coupling_cols[section].reshape(SECTION, COUPLED)
        solved_parts = []
        rounded_parts = []
        for current in range(PANELS):
            rows_now = slice(current * PANEL, (current + 1) * PANEL)
            panel_total = jnp.zeros((PANEL, SOURCES), jnp.float32)
            for earlier in range(current):
                cols_then = slice(earlier * PANEL, (earlier + 1) * PANEL)
                panel_total = panel_total + jnp.dot(masked_cols[cols_then, rows_now].T, rounded_parts[earlier], preferred_element_type=jnp.float32)
            solved = jnp.dot(diag_inverse[section, rows_now], right_side[section, rows_now] - panel_total, precision=precise, preferred_element_type=jnp.float32)
            solved_parts.append(solved)
            rounded_parts.append(solved.astype(jnp.bfloat16))
        rounded_all = jnp.concatenate(rounded_parts, axis=0)
        onehot = (separator_ids[:, None] == separator_rows[section][None, :]).astype(jnp.float32)
        contribution = jnp.dot(coupled.T, rounded_all, preferred_element_type=jnp.float32)
        mapped_total = mapped_total + jnp.dot(onehot, contribution, precision=precise, preferred_element_type=jnp.float32)
        kept.append((section, masked_cols, coupled, onehot, solved_parts))
    root_half = jnp.dot(root_inverse, root_right - mapped_total, precision=precise, preferred_element_type=jnp.float32)
    root_solution = jnp.dot(root_inverse.T, root_half, precision=precise, preferred_element_type=jnp.float32)
    outputs = []
    for section, masked_cols, coupled, onehot, solved_parts in kept:
        picked = jnp.dot(onehot.T, root_solution, precision=precise, preferred_element_type=jnp.float32).astype(jnp.bfloat16)
        couple_back = jnp.dot(coupled, picked, preferred_element_type=jnp.float32)
        finished = [None] * PANELS
        finished_low = [None] * PANELS
        for current in range(PANELS - 1, -1, -1):
            rows_now = slice(current * PANEL, (current + 1) * PANEL)
            panel_total = couple_back[rows_now]
            for later in range(current + 1, PANELS):
                rows_later = slice(later * PANEL, (later + 1) * PANEL)
                panel_total = panel_total + jnp.dot(masked_cols[rows_now, rows_later], finished_low[later], preferred_element_type=jnp.float32)
            value = jnp.dot(diag_inverse[section, rows_now].T, solved_parts[current] - panel_total, precision=precise, preferred_element_type=jnp.float32)
            finished[current] = value
            finished_low[current] = value.astype(jnp.bfloat16)
        outputs.append(jnp.concatenate(finished, axis=0))
    return jnp.stack(outputs), root_solution
```

```python
import functools

import jax
import jax.numpy as jnp
from jax import lax
from jax.experimental import pallas as pl
from jax.experimental.pallas import tpu as pltpu
from jax.sharding import PartitionSpec as P

BLOCK = 256
F32 = jnp.float32
BF16 = jnp.bfloat16
PIECES = 2


def mm(a, b):
    return lax.dot_general(a, b, (((1,), (0,)), ((), ())), preferred_element_type=F32)


def mm_nt(a, b):
    return lax.dot_general(a, b, (((1,), (1,)), ((), ())), preferred_element_type=F32)


def halves(x):
    high = x.astype(BF16)
    low = (x - high.astype(F32)).astype(BF16)
    return high, low


def paired(x):
    return jnp.concatenate(halves(x), axis=1)


def mm_paired(high, low, pair):
    both = mm(high, pair) + mm(low, pair)
    sources = pair.shape[1] // 2
    return both[:, :sources] + both[:, sources:]


def kernel(
    sizes,
    factor_hbm,
    pattern_hbm,
    inverse_hbm,
    couple_hbm,
    rows_hbm,
    root_hbm,
    right_hbm,
    root_right_hbm,
    x_out,
    root_out,
    e_raw,
    m_raw,
    c_raw,
    r_raw,
    b_raw,
    e_hi,
    e_lo,
    et_hi,
    et_lo,
    m_mask,
    m_turn,
    spread,
    spread_turn,
    r_hi,
    r_lo,
    rt_hi,
    rt_lo,
    y_keep,
    y_low,
    y_first,
    mapped_snd,
    mapped_rcv,
    a_snd,
    a_rcv,
    a_all,
    s_snd,
    s_rcv,
    z_snd,
    z_rcv,
    rhs_hi,
    rhs_lo,
    t_snd,
    t_rcv,
    sep_low,
    root_keep,
    back_snd,
    back_rcv,
    x_all,
    give,
    take,
    load_sem,
    pair_snd,
    pair_rcv,
    col_snd,
    col_rcv,
    z_ssem,
    z_rsem,
    pattern,
    rows_ref,
    root_right,
):
    subs, cols = sizes
    sub = lax.axis_index("sub")
    row = lax.axis_index("row")
    col = lax.axis_index("col")
    width = e_raw.shape[0]
    panel = e_raw.shape[1]
    share = r_raw.shape[0]
    separator = r_raw.shape[1]

    def load(source, target, index):
        return pltpu.make_async_copy(source, target, load_sem.at[index])

    get_b = load(right_hbm.at[0], b_raw, 0)
    get_m = load(factor_hbm.at[0, 0], m_raw, 1)
    get_c = load(couple_hbm.at[0, 0], c_raw, 2)
    get_r = load(root_hbm, r_raw, 3)
    get_p = load(pattern_hbm, pattern, 4 + cols)
    get_n = load(rows_hbm, rows_ref, 5 + cols)
    get_rr = load(root_right_hbm, root_right, 6 + cols)
    get_e = []
    for k in range(cols):
        ends = pl.ds(k * width, width)
        get_e.append(load(inverse_hbm.at[0, :, ends], e_raw.at[:, ends], 4 + k))

    @pl.when(row == 0)
    def _():
        for copy in [get_b] + get_e + [get_n, get_c]:
            copy.start()

    @pl.when(row != 0)
    def _():
        for copy in [get_p, get_m, get_n] + get_e + [get_b, get_c, get_r, get_rr]:
            copy.start()

    barrier = pltpu.get_barrier_semaphore()
    pl.semaphore_signal(barrier, inc=1, device_id={"row": 1 - row})
    for d in range(1, cols):
        pl.semaphore_signal(barrier, inc=1, device_id={"col": lax.rem(col + d, cols)})
    for d in range(1, subs):
        pl.semaphore_signal(barrier, inc=1, device_id={"sub": lax.rem(sub + d, subs)})

    def ahead(d):
        return lax.rem(col + d, cols)

    def behind(d):
        return lax.rem(col + cols - d, cols)

    def part(k, size):
        return pl.ds(pl.multiple_of(k * size, size), size)

    def to_pair(source, target, index):
        return pltpu.make_async_remote_copy(
            source, target, pair_snd.at[index], pair_rcv.at[index], device_id={"row": 1 - row}
        )

    def to_col(source, target, stage, d):
        return pltpu.make_async_remote_copy(
            source, target, col_snd.at[stage, d], col_rcv.at[stage, d], device_id={"col": ahead(d)}
        )

    def rows_of(piece, size):
        return pl.ds(piece * (size // PIECES), size // PIECES)

    def piece_of(k, piece, size):
        extent = size // PIECES
        return pl.ds(pl.multiple_of(k * size + piece * extent, extent), extent)

    def scatter(make, send, receive, stage):
        size = send.shape[1]
        own, copies = [], []
        for piece in range(PIECES):
            rows = rows_of(piece, size)
            sent = []
            for d in range(1, cols):
                send[d, rows, :] = make(ahead(d), piece).astype(send.dtype)
                copy = to_col(
                    send.at[d, rows], receive.at[d, rows], stage * PIECES + piece, d
                )
                copy.start()
                sent.append(copy)
            own.append(make(col, piece))
            copies.append(sent)
        return own, copies

    def gathered(own, receive, copies, piece):
        total = own[piece]
        rows = rows_of(piece, receive.shape[1])
        for d, copy in zip(range(1, cols), copies[piece]):
            copy.wait_recv()
            total = total + receive[d, rows, :].astype(F32)
        return total

    def share_out(target, slot):
        copies = []
        for d in range(1, cols):
            copy = to_col(target, target, slot, d)
            copy.start()
            copies.append(copy)
        return copies

    def finish(copies):
        for copy in copies:
            if isinstance(copy, list):
                finish(copy)
            else:
                copy.wait_send()

    def apply_inverse():
        get_b.wait()
        total = jnp.zeros((width, b_raw.shape[1]), F32)
        for k in range(cols):
            get_e[k].wait()
            high, low = halves(e_raw[:, k * width : (k + 1) * width])
            e_hi[k] = high
            e_lo[k] = low
            pair = paired(b_raw[k * width : (k + 1) * width, :])
            total = total + mm_paired(high, low, pair)
        return total

    def turn_inverse():
        for k in range(cols):
            et_hi[k], et_lo[k] = halves(e_raw[:, k * width : (k + 1) * width].T)

    step = min(BLOCK, separator)

    def hits(first):
        at = lax.broadcasted_iota(jnp.int32, (step, rows_ref.shape[1]), 0) + first
        return jnp.where(at == rows_ref[...], 1.0, 0.0).astype(BF16)

    def make_spread():
        for first in range(0, separator, step):
            spread[first : first + step, :] = mm_nt(hits(first), c_raw[...]).astype(BF16)

    def make_spread_turn():
        for first in range(0, separator, step):
            spread_turn[:, first : first + step] = mm_nt(c_raw[...], hits(first)).astype(BF16)

    @pl.when(row == 0)
    def _():
        value = apply_inverse()
        y_keep[...] = value
        y_low[...] = value.astype(BF16)

    @pl.when(row != 0)
    def _():
        tall = min(width, BLOCK)
        get_p.wait()
        get_m.wait()
        for at in range(0, width, tall):
            column = (col * width + at) // BLOCK
            for block in range(panel // BLOCK):
                present = pattern[0, panel // BLOCK + block, column].astype(F32)
                ends = slice(block * BLOCK, (block + 1) * BLOCK)
                kept = m_raw[at : at + tall, ends].astype(F32) * present
                m_raw[at : at + tall, ends] = kept.astype(BF16)
        for k in range(cols):
            piece = m_raw[:, k * width : (k + 1) * width]
            m_mask[k] = piece
            m_turn[k] = piece.astype(F32).T.astype(BF16)

    pl.semaphore_wait(barrier, 1 + (cols - 1) + (subs - 1))

    def turned(pair):
        def make(k, piece):
            rows = rows_of(piece, width)
            return mm_paired(et_hi[k, rows, :], et_lo[k, rows, :], pair)

        return make

    @pl.when(row == 0)
    def _():
        first = to_pair(y_low, y_first, 0)
        first.start()
        get_c.wait()
        get_n.wait()
        make_spread()
        mapped_snd[...] = mm(spread[...], y_low[...])
        second = to_pair(mapped_snd, mapped_rcv, 1)
        second.start()
        make_spread_turn()
        turn_inverse()
        to_pair(sep_low, sep_low, 2).wait_recv()
        y_keep[...] = y_keep[...] - mm(spread_turn[...], sep_low[...])
        to_pair(root_keep, root_keep, 3).wait_recv()
        root_out[...] = root_keep[...]
        to_pair(give, take, 4).wait_recv()
        pair = paired(y_keep[...] - take[...])
        own, copies = scatter(turned(pair), back_snd, back_rcv, 7)
        for piece in range(PIECES):
            x_out[0, rows_of(piece, width), :] = gathered(own, back_rcv, copies, piece)
        finish(copies + [first, second])

    @pl.when(row != 0)
    def _():
        to_pair(y_low, y_first, 0).wait_recv()
        low = y_first[...]
        own, sends_a = scatter(
            lambda k, piece: mm(m_turn[k, rows_of(piece, width), :], low), a_snd, a_rcv, 0
        )
        started = apply_inverse()
        sends_b = []
        for piece in range(PIECES):
            rows = rows_of(piece, width)
            a_all[col, rows, :] = gathered(own, a_rcv, sends_a, piece).astype(BF16)
            sends_b.append(share_out(a_all.at[col, rows], PIECES + piece))
        get_c.wait()
        get_n.wait()
        make_spread()
        value = started
        for d in range(cols):
            k = behind(d)
            if d > 0:
                for piece in range(PIECES):
                    sends_b[piece][d - 1].wait_recv()
            value = value - (mm(e_hi[k], a_all[k]) + mm(e_lo[k], a_all[k]))
        y_keep[...] = value
        own_low = value.astype(BF16)
        to_pair(mapped_snd, mapped_rcv, 1).wait_recv()

        def separator_rows(k, piece):
            rows = piece_of(k, piece, share)
            return mm(spread[rows, :], own_low) + mapped_rcv[rows, :]

        own, sends_c = scatter(separator_rows, s_snd, s_rcv, 2)
        get_r.wait()
        get_rr.wait()
        r_hi[...], r_lo[...] = halves(r_raw[...])
        for first in range(0, separator, step):
            ends = slice(first, first + step)
            rt_hi[ends, :], rt_lo[ends, :] = halves(r_raw[:, ends].T)
        sends_z = []
        for piece in range(PIECES):
            rows = rows_of(piece, share)
            own[piece] = gathered(own, s_rcv, sends_c, piece)
            z_snd[rows, :] = own[piece].astype(BF16)
            sent = []
            for d in range(1, subs):
                copy = pltpu.make_async_remote_copy(
                    z_snd.at[rows],
                    z_rcv.at[d, rows],
                    z_ssem.at[piece, d],
                    z_rsem.at[piece, d],
                    device_id={"sub": lax.rem(sub + d, subs)},
                )
                copy.start()
                sent.append(copy)
            sends_z.append(sent)
        make_spread_turn()
        turn_inverse()
        sends_d = []
        for piece in range(PIECES):
            rows = rows_of(piece, share)
            total = own[piece]
            for d, copy in zip(range(1, subs), sends_z[piece]):
                copy.wait_recv()
                total = total + z_rcv[d, rows, :].astype(F32)
            high, low = halves(root_right[rows, :] - total)
            place = piece_of(col, piece, share)
            rhs_hi[place, :] = high
            rhs_lo[place, :] = low
            sends_d.append(share_out(rhs_hi.at[place], 3 * PIECES + piece))
        rest = share_out(rhs_lo.at[part(col, share)], 4 * PIECES)
        for sent in sends_d:
            for copy in sent:
                copy.wait_recv()
        half = mm(r_hi[...], rhs_hi[...]) + mm(r_lo[...], rhs_hi[...])
        for copy in rest:
            copy.wait_recv()
        pair_r = paired(half + mm(r_hi[...], rhs_lo[...]))

        def root_rows(k, piece):
            rows = piece_of(k, piece, share)
            return mm_paired(rt_hi[rows, :], rt_lo[rows, :], pair_r)

        own, sends_e = scatter(root_rows, t_snd, t_rcv, 5)
        sends_f = []
        for piece in range(PIECES):
            total = gathered(own, t_rcv, sends_e, piece)
            place = piece_of(col, piece, share)
            sep_low[place, :] = total.astype(BF16)
            sends_f.append(share_out(sep_low.at[place], 6 * PIECES + piece))
            root_out[rows_of(piece, share), :] = total
            root_keep[rows_of(piece, share), :] = total
        third = to_pair(root_keep, root_keep, 3)
        third.start()
        for sent in sends_f:
            for copy in sent:
                copy.wait_recv()
        fourth = to_pair(sep_low, sep_low, 2)
        fourth.start()
        pair = paired(y_keep[...] - mm(spread_turn[...], sep_low[...]))
        own, sends_g = scatter(turned(pair), back_snd, back_rcv, 7)
        sends_h = []
        for piece in range(PIECES):
            rows = rows_of(piece, width)
            total = gathered(own, back_rcv, sends_g, piece)
            x_all[col, rows, :] = total.astype(BF16)
            sends_h.append(share_out(x_all.at[col, rows], 8 * PIECES + piece))
            x_out[0, rows, :] = total
        total = jnp.zeros(give.shape, F32)
        for d in range(cols):
            k = behind(d)
            if d > 0:
                for piece in range(PIECES):
                    sends_h[piece][d - 1].wait_recv()
            total = total + mm(m_mask[k], x_all[k])
        give[...] = total
        fifth = to_pair(give, take, 4)
        fifth.start()
        finish([sends_a, sends_b, sends_c, sends_z, sends_d, rest, sends_e, sends_f])
        finish([sends_g, sends_h, third, fourth, fifth])


def shards(
    sizes,
    factor_cols,
    block_pattern,
    diag_inverse,
    coupling_cols,
    separator_rows,
    root_inverse,
    right_side,
    root_right,
):
    subs, cols = sizes
    width, panel = diag_inverse.shape[1:]
    share, separator = root_inverse.shape
    sources = right_side.shape[2]
    coupled = coupling_cols.shape[3]
    hbm = pl.BlockSpec(memory_space=pltpu.HBM)
    vmem = pl.BlockSpec(memory_space=pltpu.VMEM)
    smem = pl.BlockSpec(memory_space=pltpu.SMEM)
    V = pltpu.VMEM
    tile = (cols, width, width)
    scratch = [
        V((width, panel), F32),
        V((width, panel), BF16),
        V((width, coupled), BF16),
        V((share, separator), F32),
        V((panel, sources), F32),
        V(tile, BF16),
        V(tile, BF16),
        V(tile, BF16),
        V(tile, BF16),
        V(tile, BF16),
        V(tile, BF16),
        V((separator, width), BF16),
        V((width, separator), BF16),
        V((share, separator), BF16),
        V((share, separator), BF16),
        V((separator, share), BF16),
        V((separator, share), BF16),
        V((width, sources), F32),
        V((width, sources), BF16),
        V((width, sources), BF16),
        V((separator, sources), F32),
        V((separator, sources), F32),
        V((cols, width, sources), BF16),
        V((cols, width, sources), BF16),
        V((cols, width, sources), BF16),
        V((cols, share, sources), BF16),
        V((cols, share, sources), BF16),
        V((share, sources), BF16),
        V((subs, share, sources), BF16),
        V((separator, sources), BF16),
        V((separator, sources), BF16),
        V((cols, share, sources), BF16),
        V((cols, share, sources), BF16),
        V((separator, sources), BF16),
        V((share, sources), F32),
        V((cols, width, sources), BF16),
        V((cols, width, sources), BF16),
        V((cols, width, sources), BF16),
        V((width, sources), F32),
        V((width, sources), F32),
        pltpu.SemaphoreType.DMA((7 + cols,)),
        pltpu.SemaphoreType.DMA((5,)),
        pltpu.SemaphoreType.DMA((5,)),
        pltpu.SemaphoreType.DMA((10 * PIECES, cols)),
        pltpu.SemaphoreType.DMA((10 * PIECES, cols)),
        pltpu.SemaphoreType.DMA((PIECES, subs)),
        pltpu.SemaphoreType.DMA((PIECES, subs)),
        pltpu.SMEM(block_pattern.shape, jnp.int32),
        V(separator_rows.shape, jnp.int32),
        V(root_right.shape, F32),
    ]
    x, root = pl.pallas_call(
        functools.partial(kernel, sizes),
        out_shape=(
            jax.ShapeDtypeStruct((1, width, sources), F32),
            jax.ShapeDtypeStruct((share, sources), F32),
        ),
        in_specs=[hbm] * 8,
        out_specs=(vmem, vmem),
        scratch_shapes=scratch,
        compiler_params=pltpu.CompilerParams(
            collective_id=0, has_side_effects=True, vmem_limit_bytes=52 * 1024 * 1024
        ),
        name="tree_solve",
    )(*[pltpu.with_memory_space_constraint(v, pltpu.HBM) for v in (
        factor_cols,
        block_pattern,
        diag_inverse,
        coupling_cols,
        separator_rows,
        root_inverse,
        right_side,
        root_right,
    )])
    return pl.pallas_call(
        publish,
        out_shape=(
            jax.ShapeDtypeStruct((1, width, sources), F32),
            jax.ShapeDtypeStruct((share, sources), F32),
        ),
        in_specs=[vmem, vmem],
        out_specs=(hbm, hbm),
        scratch_shapes=[pltpu.SemaphoreType.DMA((2,))],
        compiler_params=pltpu.CompilerParams(vmem_limit_bytes=2 * 1024 * 1024),
        name="publish",
    )(x, root)


def publish(x, root, x_out, root_out, sem):
    outs = [pltpu.make_async_copy(x, x_out, sem.at[0]), pltpu.make_async_copy(root, root_out, sem.at[1])]
    for out in outs:
        out.start()
    for out in outs:
        out.wait()


def solution(mesh):
    sizes = (mesh.shape["sub"], mesh.shape["col"])
    return jax.shard_map(
        functools.partial(shards, sizes),
        mesh=mesh,
        in_specs=(
            P("sub", None, "col", "row"),
            P("sub", None, None),
            P("sub", ("row", "col"), None),
            P("sub", "row", "col", None),
            P("sub", None),
            P("col", None),
            P("sub", "row", None),
            P("col", None),
        ),
        out_specs=(P("sub", ("row", "col"), None), P("col", None)),
        check_vma=False,
    )
```

```python
import functools

import jax
import jax.numpy as jnp
from jax import lax
from jax.experimental import pallas as pl
from jax.experimental.pallas import tpu as pltpu
from jax.sharding import PartitionSpec as P

BLOCK = 256
F32 = jnp.float32
BF16 = jnp.bfloat16
CHUNKS = 2
SLOTS = 4


def mm(a, b):
    return lax.dot_general(a, b, (((1,), (0,)), ((), ())), preferred_element_type=F32)


def mm_nt(a, b):
    return lax.dot_general(a, b, (((1,), (1,)), ((), ())), preferred_element_type=F32)


def halves(x):
    high = x.astype(BF16)
    low = (x - high.astype(F32)).astype(BF16)
    return high, low


def paired(x):
    return jnp.concatenate(halves(x), axis=1)


def mm_paired(high, low, pair):
    both = mm(high, pair) + mm(low, pair)
    sources = pair.shape[1] // 2
    return both[:, :sources] + both[:, sources:]


def divided(size, most):
    count = most
    while count > 1 and size % (16 * count):
        count //= 2
    return count


def offsets(cols):
    tall = max(s for s in range(1, cols + 1) if s * s <= cols and cols % s == 0)
    wide = cols // tall
    steps = [(y, x) for y in range(tall) for x in range(wide)]

    def hops(step):
        return min(step[0], tall - step[0]) + min(step[1], wide - step[1])

    far = sorted(steps[1:], key=lambda step: (-hops(step), -step[0], -step[1]))
    return tall, wide, [(0, 0)] + far


def kernel(
    sizes,
    factor_hbm,
    pattern_hbm,
    inverse_hbm,
    couple_hbm,
    rows_hbm,
    root_hbm,
    right_hbm,
    root_right_hbm,
    x_out,
    root_out,
    e_raw,
    m_raw,
    c_raw,
    r_raw,
    b_raw,
    b_pair,
    w_pair,
    e_hi,
    e_lo,
    et_hi,
    et_lo,
    m_turn,
    spread,
    spread_turn,
    r_hi,
    r_lo,
    rt_hi,
    rt_lo,
    y_keep,
    y_low,
    mapped_snd,
    mapped_rcv,
    part_own,
    part_snd,
    a_rcv,
    a_all,
    s_rcv,
    z_snd,
    z_rcv,
    rhs_hi,
    rhs_lo,
    t_rcv,
    sep_low,
    root_keep,
    back_rcv,
    x_all,
    pattern,
    rows_ref,
    root_right,
    load_sem,
    pair_snd,
    pair_rcv,
    col_snd,
    col_rcv,
    z_ssem,
    z_rsem,
):
    subs, cols = sizes
    sub = lax.axis_index("sub")
    row = lax.axis_index("row")
    col = lax.axis_index("col")
    width = e_raw.shape[0]
    panel = e_raw.shape[1]
    share = r_raw.shape[0]
    separator = r_raw.shape[1]
    tall, wide, steps = offsets(cols)
    col_y = lax.div(col, wide)
    col_x = lax.rem(col, wide)

    def ahead(i):
        y, x = steps[i]
        return lax.rem(col_y + y, tall) * wide + lax.rem(col_x + x, wide)

    def behind(i):
        y, x = steps[i]
        return lax.rem(col_y + (tall - y), tall) * wide + lax.rem(col_x + (wide - x), wide)

    def load(source, target, index):
        return pltpu.make_async_copy(source, target, load_sem.at[index])

    thick = width // CHUNKS
    get_b = load(right_hbm.at[0], b_raw, 0)
    get_m = load(factor_hbm.at[0, 0], m_raw, 1)
    get_c = load(couple_hbm.at[0, 0], c_raw, 2)
    get_r = load(root_hbm, r_raw, 3)
    get_p = load(pattern_hbm, pattern, 4)
    get_n = load(rows_hbm, rows_ref, 5)
    get_rr = load(root_right_hbm, root_right, 6)
    get_e = []
    for c in range(CHUNKS):
        rows = pl.ds(c * thick, thick)
        get_e.append(load(inverse_hbm.at[0, rows], e_raw.at[rows], 7 + c))

    @pl.when(row == 0)
    def _():
        for copy in [get_b] + get_e + [get_n, get_c]:
            copy.start()

    @pl.when(row != 0)
    def _():
        for copy in [get_p, get_m, get_n, get_c, get_b] + get_e + [get_r, get_rr]:
            copy.start()

    barrier = pltpu.get_barrier_semaphore()
    pl.semaphore_signal(barrier, inc=1, device_id={"row": 1 - row})
    for i in range(1, cols):
        pl.semaphore_signal(barrier, inc=1, device_id={"col": ahead(i)})
        pl.semaphore_signal(barrier, inc=1, device_id={"row": 1 - row, "col": ahead(i)})
    for d in range(1, subs):
        pl.semaphore_signal(barrier, inc=1, device_id={"sub": lax.rem(sub + d, subs)})

    def greet():
        pl.semaphore_wait(barrier, 1 + 2 * (cols - 1) + (subs - 1))

    def part(k, size):
        return pl.ds(pl.multiple_of(k * size, size), size)

    def to_pair(source, target, index):
        return pltpu.make_async_remote_copy(
            source, target, pair_snd.at[index], pair_rcv.at[index], device_id={"row": 1 - row}
        )

    def to_col(source, target, slot, i):
        return pltpu.make_async_remote_copy(
            source, target, col_snd.at[slot // SLOTS], col_rcv.at[slot, i], device_id={"col": ahead(i)}
        )

    def to_other(source, target, slot, i):
        return pltpu.make_async_remote_copy(
            source,
            target,
            col_snd.at[slot // SLOTS],
            col_rcv.at[slot, i],
            device_id={"row": 1 - row, "col": ahead(i)},
        )

    def scatter(make, size, receive, segments, pieces):
        pieces = divided(size, pieces)
        segments = min(segments, pieces)
        extent = size // segments
        fine = size // pieces
        copies = []
        for segment in range(segments):
            rows = pl.ds(segment * extent, extent)
            for i in range(1, cols):
                value = make(i, ahead(i), segment * extent, extent)
                part_snd[i, rows, :] = value.astype(BF16)
            part_own[rows, :] = make(0, col, segment * extent, extent)
            for piece in range(pieces // segments):
                at = pl.ds(segment * extent + piece * fine, fine)
                slot = len(copies)
                sent = []
                for i in range(1, cols):
                    copy = to_col(part_snd.at[i, at], receive.at[i, at], slot, i)
                    copy.start()
                    sent.append(copy)
                copies.append((at, sent))
        return copies

    def gathered(receive, at, sent):
        for copy in sent:
            copy.wait_recv()
        total = part_own[at, :]
        for i in range(1, cols):
            total = total + receive[i, at, :].astype(F32)
        return total

    def share_out(target, slot):
        copies = []
        for i in range(1, cols):
            copy = to_col(target, target, slot, i)
            copy.start()
            copies.append(copy)
        return copies

    def sent_out(kind, first, size):
        block = part_snd.at[pl.ds(first, cols - first), pl.ds(0, size)]
        pltpu.make_async_remote_copy(
            block, block, col_snd.at[kind], col_rcv.at[0, 0], device_id={"row": 1 - row}
        ).wait_send()

    def sent_across():
        block = z_rcv.at[pl.ds(1, subs - 1)]
        pltpu.make_async_remote_copy(
            block, block, z_ssem.at[0], z_rsem.at[0, 0], device_id={"row": 1 - row}
        ).wait_send()

    def finish(copies):
        for copy in copies:
            copy.wait_send()

    def apply_inverse(c, put):
        rows = pl.ds(c * thick, thick)
        high, low = halves(e_raw[rows, :])
        e_hi[rows, :] = high
        e_lo[rows, :] = low
        put(rows, mm_paired(high, low, b_pair[...]))

    def turn_inverse():
        for i in range(cols):
            block = e_raw[:, part(ahead(i), width)]
            et_hi[i], et_lo[i] = halves(block.T)

    step = min(BLOCK, separator)

    def hits(first):
        at = lax.broadcasted_iota(jnp.int32, (step, rows_ref.shape[1]), 0) + first
        return jnp.where(at == rows_ref[...], 1.0, 0.0).astype(BF16)

    def make_spread():
        for first in range(0, separator, step):
            spread[first : first + step, :] = mm_nt(hits(first), c_raw[...]).astype(BF16)

    def make_spread_turn():
        for first in range(0, separator, step):
            spread_turn[:, first : first + step] = mm_nt(c_raw[...], hits(first)).astype(BF16)

    def turned(i, k, start, extent):
        rows = pl.ds(start, extent)
        return mm_paired(et_hi[i, rows, :], et_lo[i, rows, :], w_pair[0:width, :])

    y_parts = []
    for c in range(CHUNKS):
        rows = pl.ds(c * thick, thick)
        y_parts.append(to_pair(y_low.at[rows], y_low.at[rows], 4 + c))
    m_whole = to_pair(m_raw, m_raw, 0)
    mapped_whole = to_pair(mapped_snd, mapped_rcv, 1)
    sep_whole = to_pair(sep_low, sep_low, 2)
    root_whole = to_pair(root_keep, root_keep, 3)

    @pl.when(row == 0)
    def _():
        def put(rows, value):
            y_keep[rows, :] = value
            y_low[rows, :] = value.astype(BF16)

        get_b.wait()
        b_pair[...] = paired(b_raw[...])
        for c in range(CHUNKS):
            get_e[c].wait()
            apply_inverse(c, put)
            if c == 0:
                greet()
            y_parts[c].start()
        get_c.wait()
        get_n.wait()
        make_spread()
        mapped_snd[...] = mm(spread[...], y_low[...])
        mapped_whole.start()
        make_spread_turn()
        turn_inverse()
        sep_whole.wait_recv()
        y_keep[...] = y_keep[...] - mm(spread_turn[...], sep_low[...])
        root_whole.wait_recv()
        root_out[...] = root_keep[...]
        m_whole.wait_recv()
        count = divided(width, 4)
        fine = width // count
        near = [0] + list(range(2, cols))
        for group in (near, [1]):
            for i in group:
                for piece in range(count):
                    at = pl.ds(piece * fine, fine)
                    to_other(
                        x_all.at[i, at], x_all.at[i, at], SLOTS + piece, i
                    ).wait_recv()
            total = y_keep[...]
            for i in group:
                total = total - mm(m_raw[:, part(behind(i), width)], x_all[i])
            if group is near:
                y_keep[...] = total
            else:
                w_pair[0:width, :] = paired(total)
        sends = scatter(turned, width, back_rcv, 2, 4)
        for at, sent in sends:
            x_out[0, at, :] = gathered(back_rcv, at, sent)
        sent_out(0, 1, width)
        finish(y_parts + [mapped_whole])

    @pl.when(row != 0)
    def _():
        high_rows = min(width, BLOCK)
        get_p.wait()
        get_m.wait()
        for at in range(0, width, high_rows):
            column = lax.div(col * width + at, BLOCK)
            for block in range(panel // BLOCK):
                present = pattern[0, panel // BLOCK + block, column].astype(F32)
                ends = slice(block * BLOCK, (block + 1) * BLOCK)
                kept = m_raw[at : at + high_rows, ends].astype(F32) * present
                m_raw[at : at + high_rows, ends] = kept.astype(BF16)
        greet()
        m_whole.start()
        for i in range(cols):
            block = m_raw[:, part(ahead(i), width)]
            m_turn[i] = block.astype(F32).T.astype(BF16)
        rhs_lo[...] = jnp.zeros(rhs_lo.shape, BF16)
        get_c.wait()
        get_n.wait()
        make_spread()
        for copy in y_parts:
            copy.wait_recv()

        def a_rows(i, k, start, extent):
            return mm(m_turn[i, pl.ds(start, extent), :], y_low[...])

        sends_a = scatter(a_rows, width, a_rcv, 2, 4)

        def put(rows, value):
            y_keep[rows, :] = value

        get_b.wait()
        b_pair[...] = paired(b_raw[...])
        for copy in get_e:
            copy.wait()
        for c in range(CHUNKS):
            apply_inverse(c, put)
        sends_b = []
        for at, sent in sends_a:
            a_all[col, at, :] = gathered(a_rcv, at, sent).astype(BF16)
            sends_b.append(share_out(a_all.at[col, at], SLOTS + len(sends_b)))
        make_spread_turn()
        for group in ([0] + list(range(2, cols)), [1]):
            for i in group:
                if i > 0:
                    for sent in sends_b:
                        sent[i - 1].wait_recv()
            total = y_keep[...]
            for i in group:
                k = behind(i)
                ends = part(k, width)
                total = total - (mm(e_hi[:, ends], a_all[k]) + mm(e_lo[:, ends], a_all[k]))
            y_keep[...] = total
        y_low[...] = y_keep[...].astype(BF16)
        mapped_whole.wait_recv()

        def separator_rows(i, k, start, extent):
            place = pl.ds(pl.multiple_of(k * share + start, 16), extent)
            return mm(spread[place, :], y_low[...]) + mapped_rcv[place, :]

        sent_out(0, 1, width)
        sends_c = scatter(separator_rows, share, s_rcv, 2, 4)
        get_r.wait()
        get_rr.wait()
        r_hi[...], r_lo[...] = halves(r_raw[...])
        for first in range(0, separator, step):
            ends = slice(first, first + step)
            rt_hi[ends, :], rt_lo[ends, :] = halves(r_raw[:, ends].T)
        sends_z = []
        for piece, (at, sent) in enumerate(sends_c):
            total = gathered(s_rcv, at, sent)
            part_own[at, :] = total
            z_snd[at, :] = total.astype(BF16)
            copies = []
            for d in range(1, subs):
                copy = pltpu.make_async_remote_copy(
                    z_snd.at[at],
                    z_rcv.at[d, at],
                    z_ssem.at[0],
                    z_rsem.at[piece, d - 1],
                    device_id={"sub": lax.rem(sub + d, subs)},
                )
                copy.start()
                copies.append(copy)
            sends_z.append((at, copies))
        turn_inverse()
        sent_out(1, 1, width)
        sends_d = []
        fine = share // len(sends_z)
        for piece, (at, copies) in enumerate(sends_z):
            for copy in copies:
                copy.wait_recv()
            total = part_own[at, :]
            for d in range(1, subs):
                total = total + z_rcv[d, at, :].astype(F32)
            high, low = halves(root_right[at, :] - total)
            place = pl.ds(pl.multiple_of(col * share + piece * fine, 16), fine)
            rhs_hi[place, :] = high
            rhs_lo[place, :] = low
            sends_d.append(share_out(rhs_hi.at[place], SLOTS + piece))
        own_half = mm(r_hi[...], rhs_lo[...])
        part_own[0:share, :] = own_half
        for sent in sends_d:
            for copy in sent:
                copy.wait_recv()
        half = mm(r_hi[...], rhs_hi[...]) + mm(r_lo[...], rhs_hi[...])
        w_pair[0:share, :] = paired(half + part_own[0:share, :])

        def root_rows(i, k, start, extent):
            place = pl.ds(pl.multiple_of(k * share + start, 16), extent)
            return mm_paired(rt_hi[place, :], rt_lo[place, :], w_pair[0:share, :])

        sent_out(0, 1, share)
        sends_e = scatter(root_rows, share, t_rcv, 2, 2)
        sent_out(1, 1, share)
        sends_f = []
        fine = share // len(sends_e)
        for piece, (at, sent) in enumerate(sends_e):
            total = gathered(t_rcv, at, sent)
            place = pl.ds(pl.multiple_of(col * share + piece * fine, 16), fine)
            sep_low[place, :] = total.astype(BF16)
            sends_f.append(share_out(sep_low.at[place], SLOTS + piece))
            root_out[at, :] = total
            root_keep[at, :] = total
        root_whole.start()
        for sent in sends_f:
            for copy in sent:
                copy.wait_recv()
        sep_whole.start()
        w_pair[0:width, :] = paired(y_keep[...] - mm(spread_turn[...], sep_low[...]))
        sent_out(0, 1, share)
        sends_g = scatter(turned, width, back_rcv, 2, 4)
        sent_out(1, 1, share)
        for piece, (at, sent) in enumerate(sends_g):
            total = gathered(back_rcv, at, sent)
            y_low[at, :] = total.astype(BF16)
            for i in list(range(1, cols)) + [0]:
                copy = to_other(y_low.at[at], x_all.at[i, at], SLOTS + piece, i)
                copy.start()
            x_out[0, at, :] = total
        sent_across()
        sent_out(0, 1, width)
        sent_out(1, 0, width)
        finish([m_whole, root_whole, sep_whole])


def publish(x, root, x_out, root_out, sem):
    copies = [
        pltpu.make_async_copy(x, x_out, sem.at[0]),
        pltpu.make_async_copy(root, root_out, sem.at[1]),
    ]
    for copy in copies:
        copy.start()
    for copy in copies:
        copy.wait()


def shards(
    sizes,
    factor_cols,
    block_pattern,
    diag_inverse,
    coupling_cols,
    separator_rows,
    root_inverse,
    right_side,
    root_right,
):
    subs, cols = sizes
    width, panel = diag_inverse.shape[1:]
    share, separator = root_inverse.shape
    sources = right_side.shape[2]
    coupled = coupling_cols.shape[3]
    hbm = pl.BlockSpec(memory_space=pltpu.HBM)
    vmem = pl.BlockSpec(memory_space=pltpu.VMEM)
    V = pltpu.VMEM
    DMA = pltpu.SemaphoreType.DMA
    tile = (cols, width, width)
    most = max(width, share)
    scratch = [
        V((width, panel), F32),
        V((width, panel), BF16),
        V((width, coupled), BF16),
        V((share, separator), F32),
        V((panel, sources), F32),
        V((panel, 2 * sources), BF16),
        V((most, 2 * sources), BF16),
        V((width, panel), BF16),
        V((width, panel), BF16),
        V(tile, BF16),
        V(tile, BF16),
        V(tile, BF16),
        V((separator, width), BF16),
        V((width, separator), BF16),
        V((share, separator), BF16),
        V((share, separator), BF16),
        V((separator, share), BF16),
        V((separator, share), BF16),
        V((width, sources), F32),
        V((width, sources), BF16),
        V((separator, sources), F32),
        V((separator, sources), F32),
        V((most, sources), F32),
        V((cols, most, sources), BF16),
        V((cols, width, sources), BF16),
        V((cols, width, sources), BF16),
        V((cols, share, sources), BF16),
        V((share, sources), BF16),
        V((subs, share, sources), BF16),
        V((separator, sources), BF16),
        V((separator, sources), BF16),
        V((cols, share, sources), BF16),
        V((separator, sources), BF16),
        V((share, sources), F32),
        V((cols, width, sources), BF16),
        V((cols, width, sources), BF16),
        pltpu.SMEM(block_pattern.shape, jnp.int32),
        V(separator_rows.shape, jnp.int32),
        V(root_right.shape, F32),
        DMA((7 + CHUNKS,)),
        DMA((4 + CHUNKS,)),
        DMA((4 + CHUNKS,)),
        DMA((2,)),
        DMA((2 * SLOTS, cols)),
        DMA((1,)),
        DMA((SLOTS, subs - 1)),
    ]
    inputs = (
        factor_cols,
        block_pattern,
        diag_inverse,
        coupling_cols,
        separator_rows,
        root_inverse,
        right_side,
        root_right,
    )
    shapes = (
        jax.ShapeDtypeStruct((1, width, sources), F32),
        jax.ShapeDtypeStruct((share, sources), F32),
    )
    x, root = pl.pallas_call(
        functools.partial(kernel, sizes),
        out_shape=shapes,
        in_specs=[hbm] * 8,
        out_specs=(vmem, vmem),
        scratch_shapes=scratch,
        compiler_params=pltpu.CompilerParams(
            collective_id=0, has_side_effects=True, vmem_limit_bytes=52 * 1024 * 1024
        ),
        name="tree_solve",
    )(*[pltpu.with_memory_space_constraint(value, pltpu.HBM) for value in inputs])
    return pl.pallas_call(
        publish,
        out_shape=shapes,
        in_specs=[vmem, vmem],
        out_specs=(hbm, hbm),
        scratch_shapes=[DMA((2,))],
        compiler_params=pltpu.CompilerParams(vmem_limit_bytes=2 * 1024 * 1024),
        name="publish",
    )(x, root)


def solution(mesh):
    sizes = (mesh.shape["sub"], mesh.shape["col"])
    return jax.shard_map(
        functools.partial(shards, sizes),
        mesh=mesh,
        in_specs=(
            P("sub", None, "col", "row"),
            P("sub", None, None),
            P("sub", ("row", "col"), None),
            P("sub", "row", "col", None),
            P("sub", None),
            P("col", None),
            P("sub", "row", None),
            P("col", None),
        ),
        out_specs=(P("sub", ("row", "col"), None), P("col", None)),
        check_vma=False,
    )
```

```python
import functools

import jax
import jax.numpy as jnp
from jax import lax
from jax.experimental import pallas as pl
from jax.experimental.pallas import tpu as pltpu
from jax.sharding import PartitionSpec as P

BLOCK = 256
F32 = jnp.float32
BF16 = jnp.bfloat16
CHUNKS = 2
SLOTS = 4


def mm(a, b):
    return lax.dot_general(a, b, (((1,), (0,)), ((), ())), preferred_element_type=F32)


def mm_nt(a, b):
    return lax.dot_general(a, b, (((1,), (1,)), ((), ())), preferred_element_type=F32)


def halves(x):
    high = x.astype(BF16)
    low = (x - high.astype(F32)).astype(BF16)
    return high, low


def paired(x):
    return jnp.concatenate(halves(x), axis=1)


def mm_paired(high, low, pair):
    both = mm(high, pair) + mm(low, pair)
    sources = pair.shape[1] // 2
    return both[:, :sources] + both[:, sources:]


def divided(size, most):
    count = most
    while count > 1 and size % (16 * count):
        count //= 2
    return count


def offsets(cols):
    tall = max(s for s in range(1, cols + 1) if s * s <= cols and cols % s == 0)
    wide = cols // tall
    steps = [(y, x) for y in range(tall) for x in range(wide)]

    def hops(step):
        return min(step[0], tall - step[0]) + min(step[1], wide - step[1])

    far = sorted(steps[1:], key=lambda step: (-hops(step), -step[0], -step[1]))
    return tall, wide, [(0, 0)] + far


def kernel(
    sizes,
    factor_hbm,
    pattern_hbm,
    inverse_hbm,
    couple_hbm,
    rows_hbm,
    root_hbm,
    right_hbm,
    root_right_hbm,
    x_out,
    root_out,
    e_raw,
    m_raw,
    c_raw,
    r_raw,
    b_raw,
    b_pair,
    w_pair,
    e_hi,
    e_lo,
    et_hi,
    et_lo,
    m_turn,
    spread,
    spread_turn,
    r_hi,
    r_lo,
    rt_hi,
    rt_lo,
    y_keep,
    y_low,
    mapped_snd,
    mapped_rcv,
    part_own,
    part_snd,
    a_rcv,
    a_all,
    s_rcv,
    z_snd,
    z_rcv,
    rhs_hi,
    rhs_lo,
    t_rcv,
    sep_low,
    root_keep,
    back_rcv,
    x_all,
    pattern,
    rows_ref,
    root_right,
    load_sem,
    pair_snd,
    pair_rcv,
    col_snd,
    col_rcv,
    z_ssem,
    z_rsem,
):
    subs, cols = sizes
    sub = lax.axis_index("sub")
    row = lax.axis_index("row")
    col = lax.axis_index("col")
    width = e_raw.shape[0]
    panel = e_raw.shape[1]
    share = r_raw.shape[0]
    separator = r_raw.shape[1]
    tall, wide, steps = offsets(cols)
    whole_lanes = share % 128 == 0
    col_y = lax.div(col, wide)
    col_x = lax.rem(col, wide)

    def ahead(i):
        y, x = steps[i]
        return lax.rem(col_y + y, tall) * wide + lax.rem(col_x + x, wide)

    def behind(i):
        y, x = steps[i]
        return lax.rem(col_y + (tall - y), tall) * wide + lax.rem(col_x + (wide - x), wide)

    def load(source, target, index):
        return pltpu.make_async_copy(source, target, load_sem.at[index])

    thick = width // CHUNKS
    get_b = load(right_hbm.at[0], b_raw, 0)
    get_m = load(factor_hbm.at[0, 0], m_raw, 1)
    get_c = load(couple_hbm.at[0, 0], c_raw, 2)
    get_r = load(root_hbm, r_raw, 3)
    get_p = load(pattern_hbm, pattern, 4)
    get_n = load(rows_hbm, rows_ref, 5)
    get_rr = load(root_right_hbm, root_right, 6)
    get_e = []
    for c in range(CHUNKS):
        rows = pl.ds(c * thick, thick)
        get_e.append(load(inverse_hbm.at[0, rows], e_raw.at[rows], 7 + c))

    @pl.when(row == 0)
    def _():
        for copy in [get_b] + get_e + [get_n, get_c]:
            copy.start()

    @pl.when(row != 0)
    def _():
        for copy in [get_p, get_m, get_n, get_c, get_b] + get_e + [get_r, get_rr]:
            copy.start()

    barrier = pltpu.get_barrier_semaphore()
    pl.semaphore_signal(barrier, inc=1, device_id={"row": 1 - row})
    for i in range(1, cols):
        pl.semaphore_signal(barrier, inc=1, device_id={"col": ahead(i)})
        pl.semaphore_signal(barrier, inc=1, device_id={"row": 1 - row, "col": ahead(i)})
    for d in range(1, subs):
        pl.semaphore_signal(barrier, inc=1, device_id={"sub": lax.rem(sub + d, subs)})

    def greet():
        pl.semaphore_wait(barrier, 1 + 2 * (cols - 1) + (subs - 1))

    def part(k, size):
        return pl.ds(pl.multiple_of(k * size, size), size)

    def to_pair(source, target, index):
        return pltpu.make_async_remote_copy(
            source, target, pair_snd.at[index], pair_rcv.at[index], device_id={"row": 1 - row}
        )

    def to_col(source, target, kind, slot, i):
        return pltpu.make_async_remote_copy(
            source, target, col_snd.at[kind], col_rcv.at[slot], device_id={"col": ahead(i)}
        )

    def gather_slot(i):
        return SLOTS + (2 if i == 0 else 0 if i == 1 else 1)

    def to_other(source, target, i):
        return pltpu.make_async_remote_copy(
            source,
            target,
            col_snd.at[1],
            col_rcv.at[gather_slot(i)],
            device_id={"row": 1 - row, "col": ahead(i)},
        )

    def arrived(slot, first, count, start, size):
        block = part_snd.at[pl.ds(first, count), pl.ds(start, size)]
        pltpu.make_async_remote_copy(
            block, block, col_snd.at[0], col_rcv.at[slot], device_id={"row": 1 - row}
        ).wait_recv()

    def far_arrived(size):
        arrived(SLOTS, 1, 1, 0, size)

    def near_arrived(count, size):
        arrived(SLOTS + 1, 0, count, 0, size)

    def scatter(make, size, receive):
        pieces = divided(size, SLOTS)
        fine = size // pieces
        spans = [pl.ds(piece * fine, fine) for piece in range(pieces)]
        batches = [[(1, 0)]]
        for piece in range(pieces):
            batch = [(i, piece) for i in range(2, cols)] + [(0, piece)]
            if piece + 1 < pieces:
                batch.insert(0, (1, piece + 1))
            batches.append(batch)
        for batch in batches:
            for i, piece in batch:
                value = make(i, ahead(i), piece * fine, fine)
                if i > 0:
                    part_snd[i, spans[piece], :] = value.astype(BF16)
                else:
                    part_own[spans[piece], :] = value
            for i, piece in batch:
                if i > 0:
                    at = spans[piece]
                    to_col(part_snd.at[i, at], receive.at[i, at], 0, piece, i).start()
        return [(at, piece, fine) for piece, at in enumerate(spans)]

    def gathered(receive, at, slot, fine):
        arrived(slot, 1, cols - 1, 0, fine)
        total = part_own[at, :]
        for i in range(1, cols):
            total = total + receive[i, at, :].astype(F32)
        return total

    def share_out(target):
        for i in range(1, cols):
            to_col(target, target, 1, gather_slot(i), i).start()

    def sent_out(kind, first, size):
        block = part_snd.at[pl.ds(first, cols - first), pl.ds(0, size)]
        pltpu.make_async_remote_copy(
            block, block, col_snd.at[kind], col_rcv.at[0], device_id={"row": 1 - row}
        ).wait_send()

    def sent_across():
        block = z_rcv.at[pl.ds(1, subs - 1)]
        pltpu.make_async_remote_copy(
            block, block, z_ssem.at[0], z_rsem.at[0], device_id={"row": 1 - row}
        ).wait_send()

    def finish(copies):
        for copy in copies:
            copy.wait_send()

    def apply_inverse(c, put):
        rows = pl.ds(c * thick, thick)
        high, low = halves(e_raw[rows, :])
        e_hi[rows, :] = high
        e_lo[rows, :] = low
        put(rows, mm_paired(high, low, b_pair[...]))

    def turn_inverse():
        for i in range(cols):
            block = e_raw[:, part(ahead(i), width)]
            et_hi[i], et_lo[i] = halves(block.T)

    step = min(BLOCK, separator)

    def hits(first):
        at = lax.broadcasted_iota(jnp.int32, (step, rows_ref.shape[1]), 0) + first
        return jnp.where(at == rows_ref[...], 1.0, 0.0).astype(BF16)

    def make_spread():
        for first in range(0, separator, step):
            spread[first : first + step, :] = mm_nt(hits(first), c_raw[...]).astype(BF16)

    def make_spread_turn():
        for first in range(0, separator, step):
            spread_turn[:, first : first + step] = mm_nt(c_raw[...], hits(first)).astype(BF16)

    def turned(i, k, start, extent):
        rows = pl.ds(start, extent)
        return mm_paired(et_hi[i, rows, :], et_lo[i, rows, :], w_pair[0:width, :])

    y_parts = []
    for c in range(CHUNKS):
        rows = pl.ds(c * thick, thick)
        y_parts.append(to_pair(y_low.at[rows], y_low.at[rows], 4 + c))
    m_whole = to_pair(m_raw, m_raw, 0)
    mapped_whole = to_pair(mapped_snd, mapped_rcv, 1)
    sep_whole = to_pair(sep_low, sep_low, 2)
    root_whole = to_pair(root_keep, root_keep, 3)

    @pl.when(row == 0)
    def _():
        def put(rows, value):
            y_keep[rows, :] = value
            y_low[rows, :] = value.astype(BF16)

        get_b.wait()
        b_pair[...] = paired(b_raw[...])
        for c in range(CHUNKS):
            get_e[c].wait()
            apply_inverse(c, put)
            if c == 0:
                greet()
            y_parts[c].start()
        get_c.wait()
        get_n.wait()
        make_spread()
        mapped_snd[...] = mm(spread[...], y_low[...])
        mapped_whole.start()
        make_spread_turn()
        turn_inverse()
        sep_whole.wait_recv()
        y_keep[...] = y_keep[...] - mm(spread_turn[...], sep_low[...])
        root_whole.wait_recv()
        root_out[...] = root_keep[...]
        m_whole.wait_recv()
        near = list(range(2, cols))
        for group in ([0], near, [1]):
            if group is near:
                near_arrived(cols - 2, width)
            elif group[0] > 0:
                far_arrived(width)
            else:
                arrived(SLOTS + 2, 0, 1, 0, width)
            total = y_keep[...]
            for i in group:
                total = total - mm(m_raw[:, part(behind(i), width)], x_all[i])
            if group[0] != 1:
                y_keep[...] = total
            else:
                w_pair[0:width, :] = paired(total)
        sends = scatter(turned, width, back_rcv)
        for at, slot, fine in sends:
            x_out[0, at, :] = gathered(back_rcv, at, slot, fine)
        sent_out(0, 1, width)
        finish(y_parts + [mapped_whole])

    @pl.when(row != 0)
    def _():
        high_rows = min(width, BLOCK)
        get_p.wait()
        get_m.wait()
        for at in range(0, width, high_rows):
            column = lax.div(col * width + at, BLOCK)
            for block in range(panel // BLOCK):
                present = pattern[0, panel // BLOCK + block, column].astype(F32)
                ends = slice(block * BLOCK, (block + 1) * BLOCK)
                kept = m_raw[at : at + high_rows, ends].astype(F32) * present
                m_raw[at : at + high_rows, ends] = kept.astype(BF16)
        greet()
        m_whole.start()
        for i in range(cols):
            block = m_raw[:, part(ahead(i), width)]
            m_turn[i] = block.astype(F32).T.astype(BF16)
        rhs_lo[...] = jnp.zeros(rhs_lo.shape, BF16)
        get_c.wait()
        get_n.wait()
        make_spread()
        for copy in y_parts:
            copy.wait_recv()

        def a_rows(i, k, start, extent):
            return mm(m_turn[i, pl.ds(start, extent), :], y_low[...])

        sends_a = scatter(a_rows, width, a_rcv)

        def put(rows, value):
            y_keep[rows, :] = value

        get_b.wait()
        b_pair[...] = paired(b_raw[...])
        for copy in get_e:
            copy.wait()
        for c in range(CHUNKS):
            apply_inverse(c, put)
        for at, slot, fine in sends_a:
            a_all[col, at, :] = gathered(a_rcv, at, slot, fine).astype(BF16)
            share_out(a_all.at[col, at])
        make_spread_turn()
        near = list(range(2, cols))
        for group in ([0], near, [1]):
            if group is near:
                near_arrived(cols - 2, width)
            elif group[0] > 0:
                far_arrived(width)
            total = y_keep[...]
            for i in group:
                k = behind(i)
                ends = part(k, width)
                total = total - (mm(e_hi[:, ends], a_all[k]) + mm(e_lo[:, ends], a_all[k]))
            y_keep[...] = total
        y_low[...] = y_keep[...].astype(BF16)
        mapped_whole.wait_recv()

        def separator_rows(i, k, start, extent):
            place = pl.ds(pl.multiple_of(k * share + start, 16), extent)
            return mm(spread[place, :], y_low[...]) + mapped_rcv[place, :]

        sent_out(0, 1, width)
        sends_c = scatter(separator_rows, share, s_rcv)
        get_r.wait()
        get_rr.wait()
        r_hi[...], r_lo[...] = halves(r_raw[...])
        for first in range(0, separator, step):
            ends = slice(first, first + step)
            rt_hi[ends, :], rt_lo[ends, :] = halves(r_raw[:, ends].T)
        sends_z = []
        for piece, (at, slot, fine) in enumerate(sends_c):
            total = gathered(s_rcv, at, slot, fine)
            part_own[at, :] = total
            z_snd[at, :] = total.astype(BF16)
            for d in range(1, subs):
                copy = pltpu.make_async_remote_copy(
                    z_snd.at[at],
                    z_rcv.at[d, at],
                    z_ssem.at[0],
                    z_rsem.at[piece],
                    device_id={"sub": lax.rem(sub + d, subs)},
                )
                copy.start()
            sends_z.append(at)
        turn_inverse()
        sent_out(1, 1, width)
        def root_block(i):
            ends = part(behind(i), share)
            right = rhs_hi[ends, :]
            return mm(r_hi[:, ends], right) + mm(r_lo[:, ends], right)

        fine = share // len(sends_z)
        for piece, at in enumerate(sends_z):
            block = z_rcv.at[pl.ds(1, subs - 1), at]
            pltpu.make_async_remote_copy(
                block, block, z_ssem.at[0], z_rsem.at[piece], device_id={"row": 1 - row}
            ).wait_recv()
            total = part_own[at, :]
            for d in range(1, subs):
                total = total + z_rcv[d, at, :].astype(F32)
            high, low = halves(root_right[at, :] - total)
            place = pl.ds(pl.multiple_of(col * share + piece * fine, 16), fine)
            rhs_hi[place, :] = high
            rhs_lo[place, :] = low
            share_out(rhs_hi.at[place])
        if whole_lanes:
            own = part(col, share)
            part_own[0:share, :] = mm(r_hi[:, own], rhs_lo[own, :]) + root_block(0)
            near_arrived(cols - 2, share)
            near_total = part_own[0:share, :]
            for i in range(2, cols):
                near_total = near_total + root_block(i)
            part_own[0:share, :] = near_total
            far_arrived(share)
            root_half = part_own[0:share, :] + root_block(1)
        else:
            part_own[0:share, :] = mm(r_hi[...], rhs_lo[...])
            near_arrived(cols - 2, share)
            far_arrived(share)
            root_half = mm(r_hi[...], rhs_hi[...]) + mm(r_lo[...], rhs_hi[...])
            root_half = root_half + part_own[0:share, :]
        w_pair[0:share, :] = paired(root_half)

        def coupled_block(i):
            ends = part(behind(i), share)
            return mm(spread_turn[:, ends], sep_low[ends, :])

        def root_rows(i, k, start, extent):
            place = pl.ds(pl.multiple_of(k * share + start, 16), extent)
            return mm_paired(rt_hi[place, :], rt_lo[place, :], w_pair[0:share, :])

        sent_out(0, 1, share)
        sends_e = scatter(root_rows, share, t_rcv)
        sent_out(1, 1, share)
        for piece, (at, slot, fine) in enumerate(sends_e):
            total = gathered(t_rcv, at, slot, fine)
            place = pl.ds(pl.multiple_of(col * share + piece * fine, 16), fine)
            sep_low[place, :] = total.astype(BF16)
            share_out(sep_low.at[place])
            root_out[at, :] = total
            root_keep[at, :] = total
        root_whole.start()
        if whole_lanes:
            y_keep[...] = y_keep[...] - coupled_block(0)
            near_arrived(cols - 2, share)
            total = y_keep[...]
            for i in range(2, cols):
                total = total - coupled_block(i)
            y_keep[...] = total
            far_arrived(share)
            sep_whole.start()
            w_pair[0:width, :] = paired(y_keep[...] - coupled_block(1))
        else:
            near_arrived(cols - 2, share)
            far_arrived(share)
            sep_whole.start()
            w_pair[0:width, :] = paired(y_keep[...] - mm(spread_turn[...], sep_low[...]))
        sent_out(0, 1, share)
        sends_g = scatter(turned, width, back_rcv)
        sent_out(1, 1, share)
        for at, slot, fine in sends_g:
            total = gathered(back_rcv, at, slot, fine)
            y_low[at, :] = total.astype(BF16)
            for i in list(range(1, cols)) + [0]:
                to_other(y_low.at[at], x_all.at[i, at], i).start()
            x_out[0, at, :] = total
        sent_across()
        sent_out(0, 1, width)
        sent_out(1, 0, width)
        finish([m_whole, root_whole, sep_whole])


def publish(x, root, x_out, root_out, sem):
    copies = [
        pltpu.make_async_copy(x, x_out, sem.at[0]),
        pltpu.make_async_copy(root, root_out, sem.at[1]),
    ]
    for copy in copies:
        copy.start()
    for copy in copies:
        copy.wait()


def shards(
    sizes,
    factor_cols,
    block_pattern,
    diag_inverse,
    coupling_cols,
    separator_rows,
    root_inverse,
    right_side,
    root_right,
):
    subs, cols = sizes
    width, panel = diag_inverse.shape[1:]
    share, separator = root_inverse.shape
    sources = right_side.shape[2]
    coupled = coupling_cols.shape[3]
    hbm = pl.BlockSpec(memory_space=pltpu.HBM)
    vmem = pl.BlockSpec(memory_space=pltpu.VMEM)
    V = pltpu.VMEM
    DMA = pltpu.SemaphoreType.DMA
    tile = (cols, width, width)
    most = max(width, share)
    scratch = [
        V((width, panel), F32),
        V((width, panel), BF16),
        V((width, coupled), BF16),
        V((share, separator), F32),
        V((panel, sources), F32),
        V((panel, 2 * sources), BF16),
        V((most, 2 * sources), BF16),
        V((width, panel), BF16),
        V((width, panel), BF16),
        V(tile, BF16),
        V(tile, BF16),
        V(tile, BF16),
        V((separator, width), BF16),
        V((width, separator), BF16),
        V((share, separator), BF16),
        V((share, separator), BF16),
        V((separator, share), BF16),
        V((separator, share), BF16),
        V((width, sources), F32),
        V((width, sources), BF16),
        V((separator, sources), F32),
        V((separator, sources), F32),
        V((most, sources), F32),
        V((cols, most, sources), BF16),
        V((cols, width, sources), BF16),
        V((cols, width, sources), BF16),
        V((cols, share, sources), BF16),
        V((share, sources), BF16),
        V((subs, share, sources), BF16),
        V((separator, sources), BF16),
        V((separator, sources), BF16),
        V((cols, share, sources), BF16),
        V((separator, sources), BF16),
        V((share, sources), F32),
        V((cols, width, sources), BF16),
        V((cols, width, sources), BF16),
        pltpu.SMEM(block_pattern.shape, jnp.int32),
        V(separator_rows.shape, jnp.int32),
        V(root_right.shape, F32),
        DMA((7 + CHUNKS,)),
        DMA((4 + CHUNKS,)),
        DMA((4 + CHUNKS,)),
        DMA((2,)),
        DMA((SLOTS + 3,)),
        DMA((1,)),
        DMA((SLOTS,)),
    ]
    inputs = (
        factor_cols,
        block_pattern,
        diag_inverse,
        coupling_cols,
        separator_rows,
        root_inverse,
        right_side,
        root_right,
    )
    shapes = (
        jax.ShapeDtypeStruct((1, width, sources), F32),
        jax.ShapeDtypeStruct((share, sources), F32),
    )
    x, root = pl.pallas_call(
        functools.partial(kernel, sizes),
        out_shape=shapes,
        in_specs=[hbm] * 8,
        out_specs=(vmem, vmem),
        scratch_shapes=scratch,
        compiler_params=pltpu.CompilerParams(
            collective_id=0, has_side_effects=True, vmem_limit_bytes=52 * 1024 * 1024
        ),
        name="tree_solve",
    )(*[pltpu.with_memory_space_constraint(value, pltpu.HBM) for value in inputs])
    return pl.pallas_call(
        publish,
        out_shape=shapes,
        in_specs=[vmem, vmem],
        out_specs=(hbm, hbm),
        scratch_shapes=[DMA((2,))],
        compiler_params=pltpu.CompilerParams(vmem_limit_bytes=2 * 1024 * 1024),
        name="publish",
    )(x, root)


def solution(mesh):
    sizes = (mesh.shape["sub"], mesh.shape["col"])
    return jax.shard_map(
        functools.partial(shards, sizes),
        mesh=mesh,
        in_specs=(
            P("sub", None, "col", "row"),
            P("sub", None, None),
            P("sub", ("row", "col"), None),
            P("sub", "row", "col", None),
            P("sub", None),
            P("col", None),
            P("sub", "row", None),
            P("col", None),
        ),
        out_specs=(P("sub", ("row", "col"), None), P("col", None)),
        check_vma=False,
    )
```

```python
import functools

import jax
import jax.numpy as jnp
from jax import lax
from jax.experimental import pallas as pl
from jax.experimental.pallas import tpu as pltpu
from jax.sharding import PartitionSpec as P

BLOCK = 256
F32 = jnp.float32
BF16 = jnp.bfloat16
CHUNKS = 2
BLOCKS = 4
SLOTS = 8


def mm(a, b):
    return lax.dot_general(a, b, (((1,), (0,)), ((), ())), preferred_element_type=F32)


def mm_nt(a, b):
    return lax.dot_general(a, b, (((1,), (1,)), ((), ())), preferred_element_type=F32)


def halves(x):
    high = x.astype(BF16)
    low = (x - high.astype(F32)).astype(BF16)
    return high, low


def paired(x):
    return jnp.concatenate(halves(x), axis=1)


def stacked(blocks, right):
    tall = mm(jnp.concatenate(blocks, axis=0), right) if len(blocks) > 1 else mm(blocks[0], right)
    values, at = [], 0
    for block in blocks:
        values.append(tall[at : at + block.shape[0], :])
        at += block.shape[0]
    return values


def mm_split(high, low, right):
    first, second = stacked([high, low], right)
    return first + second


def folded(both):
    sources = both.shape[1] // 2
    return both[:, :sources] + both[:, sources:]


def mm_paired(high, low, pair):
    return folded(mm_split(high, low, pair))


def mm_apart(high, low, pair):
    return folded(mm(high, pair) + mm(low, pair))


def divided(size, most):
    count = most
    while count > 1 and size % (16 * count):
        count //= 2
    return count


def offsets(cols):
    tall = max(s for s in range(1, cols + 1) if s * s <= cols and cols % s == 0)
    wide = cols // tall
    steps = [(y, x) for y in range(tall) for x in range(wide)]

    def hops(step):
        return min(step[0], tall - step[0]) + min(step[1], wide - step[1])

    far = sorted(steps[1:], key=lambda step: (-hops(step), -step[0], -step[1]))
    return tall, wide, [(0, 0)] + far


def kernel(
    sizes,
    factor_hbm,
    pattern_hbm,
    inverse_hbm,
    couple_hbm,
    rows_hbm,
    root_hbm,
    right_hbm,
    root_right_hbm,
    x_out,
    root_out,
    e_raw,
    m_raw,
    c_raw,
    r_raw,
    b_raw,
    b_pair,
    w_pair,
    e_hi,
    e_lo,
    et_hi,
    et_lo,
    m_turn,
    spread,
    spread_turn,
    r_hi,
    r_lo,
    rt_hi,
    rt_lo,
    y_keep,
    y_low,
    mapped_snd,
    mapped_rcv,
    part_own,
    part_snd,
    a_rcv,
    a_all,
    s_rcv,
    z_snd,
    z_rcv,
    rhs_hi,
    rhs_lo,
    t_rcv,
    sep_low,
    root_keep,
    back_rcv,
    x_all,
    pattern,
    rows_ref,
    root_right,
    load_sem,
    pair_snd,
    pair_rcv,
    col_snd,
    col_rcv,
    z_ssem,
    z_rsem,
):
    subs, cols = sizes
    sub = lax.axis_index("sub")
    row = lax.axis_index("row")
    col = lax.axis_index("col")
    width = e_raw.shape[0]
    panel = e_raw.shape[1]
    share = r_raw.shape[0]
    separator = r_raw.shape[1]
    tall, wide, steps = offsets(cols)
    whole_lanes = share % 128 == 0
    col_y = lax.div(col, wide)
    col_x = lax.rem(col, wide)

    def ahead(i):
        y, x = steps[i]
        return lax.rem(col_y + y, tall) * wide + lax.rem(col_x + x, wide)

    def behind(i):
        y, x = steps[i]
        return lax.rem(col_y + (tall - y), tall) * wide + lax.rem(col_x + (wide - x), wide)

    def load(source, target, index):
        return pltpu.make_async_copy(source, target, load_sem.at[index])

    thick = width // CHUNKS
    get_b = load(right_hbm.at[0], b_raw, 0)
    get_m = load(factor_hbm.at[0, 0], m_raw, 1)
    get_c = load(couple_hbm.at[0, 0], c_raw, 2)
    get_r = load(root_hbm, r_raw, 3)
    get_p = load(pattern_hbm, pattern, 4)
    get_n = load(rows_hbm, rows_ref, 5)
    get_rr = load(root_right_hbm, root_right, 6)
    get_e = []
    for c in range(CHUNKS):
        rows = pl.ds(c * thick, thick)
        get_e.append(load(inverse_hbm.at[0, rows], e_raw.at[rows], 7 + c))

    @pl.when(row == 0)
    def _():
        for copy in [get_b] + get_e + [get_n, get_c]:
            copy.start()

    @pl.when(row != 0)
    def _():
        for copy in [get_p, get_m, get_n, get_c]:
            copy.start()

    barrier = pltpu.get_barrier_semaphore()
    pl.semaphore_signal(barrier, inc=1, device_id={"row": 1 - row})
    for i in range(1, cols):
        pl.semaphore_signal(barrier, inc=1, device_id={"col": ahead(i)})
        pl.semaphore_signal(barrier, inc=1, device_id={"row": 1 - row, "col": ahead(i)})
    for d in range(1, subs):
        pl.semaphore_signal(barrier, inc=1, device_id={"sub": lax.rem(sub + d, subs)})

    def greet():
        pl.semaphore_wait(barrier, 1 + 2 * (cols - 1) + (subs - 1))

    def part(k, size):
        return pl.ds(pl.multiple_of(k * size, size), size)

    def to_pair(source, target, index):
        return pltpu.make_async_remote_copy(
            source, target, pair_snd.at[index], pair_rcv.at[index], device_id={"row": 1 - row}
        )

    def to_col(source, target, kind, slot, i):
        return pltpu.make_async_remote_copy(
            source, target, col_snd.at[kind], col_rcv.at[slot], device_id={"col": ahead(i)}
        )

    def gather_slot(i):
        return SLOTS + (2 if i == 0 else 0 if i == 1 else 1)

    def to_other(source, target, i):
        return pltpu.make_async_remote_copy(
            source,
            target,
            col_snd.at[1],
            col_rcv.at[gather_slot(i)],
            device_id={"row": 1 - row, "col": ahead(i)},
        )

    def arrived(slot, first, count, start, size):
        block = part_snd.at[pl.ds(first, count), pl.ds(start, size)]
        pltpu.make_async_remote_copy(
            block, block, col_snd.at[0], col_rcv.at[slot], device_id={"row": 1 - row}
        ).wait_recv()

    def far_arrived(size):
        arrived(SLOTS, 1, 1, 0, size)

    def near_arrived(count, size):
        arrived(SLOTS + 1, 0, count, 0, size)

    def scatter(make, size, receive):
        blocks = divided(size, BLOCKS)
        pieces = divided(size, SLOTS)
        tallest = size // blocks
        fine = size // pieces
        each = pieces // blocks
        batches = [[(1, 0)]]
        for block in range(blocks):
            batch = [(i, block) for i in range(2, cols)] + [(0, block)]
            if block + 1 < blocks:
                batch.insert(0, (1, block + 1))
            batches.append(batch)
        for batch in batches:
            values = make([(i, block * tallest, tallest) for i, block in batch])
            for (i, block), value in zip(batch, values):
                rows = pl.ds(block * tallest, tallest)
                if i > 0:
                    part_snd[i, rows, :] = value.astype(BF16)
                else:
                    part_own[rows, :] = value
            for turn in range(each):
                for i, block in batch:
                    if i > 0:
                        piece = block * each + turn
                        at = pl.ds(piece * fine, fine)
                        to_col(part_snd.at[i, at], receive.at[i, at], 0, piece, i).start()
        return [(pl.ds(piece * fine, fine), piece, fine) for piece in range(pieces)]

    def gathered(receive, at, slot, fine):
        arrived(slot, 1, cols - 1, 0, fine)
        total = part_own[at, :]
        for i in range(1, cols):
            total = total + receive[i, at, :].astype(F32)
        return total

    def share_out(target):
        for i in range(1, cols):
            to_col(target, target, 1, gather_slot(i), i).start()

    def sent_out(kind, first, size):
        block = part_snd.at[pl.ds(first, cols - first), pl.ds(0, size)]
        pltpu.make_async_remote_copy(
            block, block, col_snd.at[kind], col_rcv.at[0], device_id={"row": 1 - row}
        ).wait_send()

    def sent_across():
        block = z_rcv.at[pl.ds(1, subs - 1)]
        pltpu.make_async_remote_copy(
            block, block, z_ssem.at[0], z_rsem.at[0], device_id={"row": 1 - row}
        ).wait_send()

    def finish(copies):
        for copy in copies:
            copy.wait_send()

    def apply_inverse(c, put):
        rows = pl.ds(c * thick, thick)
        high, low = halves(e_raw[rows, :])
        e_hi[rows, :] = high
        e_lo[rows, :] = low
        put(rows, mm_paired(high, low, b_pair[...]))

    def turn_inverse():
        for i in range(cols):
            block = e_raw[:, part(ahead(i), width)]
            et_hi[i], et_lo[i] = halves(block.T)

    step = min(BLOCK, separator)

    def hits(first):
        at = lax.broadcasted_iota(jnp.int32, (step, rows_ref.shape[1]), 0) + first
        return jnp.where(at == rows_ref[...], 1.0, 0.0).astype(BF16)

    def make_spread():
        for first in range(0, separator, step):
            spread[first : first + step, :] = mm_nt(hits(first), c_raw[...]).astype(BF16)

    def make_spread_turn():
        for first in range(0, separator, step):
            spread_turn[:, first : first + step] = mm_nt(c_raw[...], hits(first)).astype(BF16)

    def turned(blocks):
        values = []
        for i, start, size in blocks:
            rows = pl.ds(start, size)
            values.append(mm_paired(et_hi[i, rows, :], et_lo[i, rows, :], w_pair[0:width, :]))
        return values

    y_parts = []
    for c in range(CHUNKS):
        rows = pl.ds(c * thick, thick)
        y_parts.append(to_pair(y_low.at[rows], y_low.at[rows], 4 + c))
    m_whole = to_pair(m_raw, m_raw, 0)
    mapped_whole = to_pair(mapped_snd, mapped_rcv, 1)
    sep_whole = to_pair(sep_low, sep_low, 2)
    root_whole = to_pair(root_keep, root_keep, 3)

    @pl.when(row == 0)
    def _():
        def put(rows, value):
            y_keep[rows, :] = value
            y_low[rows, :] = value.astype(BF16)

        get_b.wait()
        b_pair[...] = paired(b_raw[...])
        for copy in get_e:
            copy.wait()
        for c in range(CHUNKS):
            apply_inverse(c, put)
        greet()
        for copy in y_parts:
            copy.start()
        get_c.wait()
        get_n.wait()
        make_spread()
        mapped_snd[...] = mm(spread[...], y_low[...])
        mapped_whole.start()
        make_spread_turn()
        turn_inverse()
        sep_whole.wait_recv()
        y_keep[...] = y_keep[...] - mm(spread_turn[...], sep_low[...])
        root_whole.wait_recv()
        root_out[...] = root_keep[...]
        m_whole.wait_recv()
        near = list(range(2, cols))
        for group in ([0], near, [1]):
            if group is near:
                near_arrived(cols - 2, width)
            elif group[0] > 0:
                far_arrived(width)
            else:
                arrived(SLOTS + 2, 0, 1, 0, width)
            total = y_keep[...]
            for i in group:
                total = total - mm(m_raw[:, part(behind(i), width)], x_all[i])
            if group[0] != 1:
                y_keep[...] = total
            else:
                w_pair[0:width, :] = paired(total)
        sends = scatter(turned, width, back_rcv)
        for at, slot, fine in sends:
            x_out[0, at, :] = gathered(back_rcv, at, slot, fine)
        sent_out(0, 1, width)
        finish(y_parts + [mapped_whole])

    @pl.when(row != 0)
    def _():
        high_rows = min(width, BLOCK)
        get_p.wait()
        get_m.wait()
        for at in range(0, width, high_rows):
            column = lax.div(col * width + at, BLOCK)
            for block in range(panel // BLOCK):
                present = pattern[0, panel // BLOCK + block, column].astype(F32)
                ends = slice(block * BLOCK, (block + 1) * BLOCK)
                kept = m_raw[at : at + high_rows, ends].astype(F32) * present
                m_raw[at : at + high_rows, ends] = kept.astype(BF16)
        greet()
        for copy in [get_b] + get_e + [get_r, get_rr]:
            copy.start()
        m_whole.start()
        for i in range(cols):
            block = m_raw[:, part(ahead(i), width)]
            m_turn[i] = block.astype(F32).T.astype(BF16)
        rhs_lo[...] = jnp.zeros(rhs_lo.shape, BF16)
        get_c.wait()
        get_n.wait()
        make_spread()
        for copy in y_parts:
            copy.wait_recv()

        def a_rows(blocks):
            rows = [m_turn[i, pl.ds(start, size), :] for i, start, size in blocks]
            return [mm(block, y_low[...]) for block in rows]

        sends_a = scatter(a_rows, width, a_rcv)

        def put(rows, value):
            y_keep[rows, :] = value

        get_b.wait()
        b_pair[...] = paired(b_raw[...])
        for copy in get_e:
            copy.wait()
        for c in range(CHUNKS):
            apply_inverse(c, put)
        for at, slot, fine in sends_a:
            a_all[col, at, :] = gathered(a_rcv, at, slot, fine).astype(BF16)
            share_out(a_all.at[col, at])
        make_spread_turn()
        near = list(range(2, cols))
        for group in ([0], near, [1]):
            if group is near:
                near_arrived(cols - 2, width)
            elif group[0] > 0:
                far_arrived(width)
            total = y_keep[...]
            for i in group:
                k = behind(i)
                ends = part(k, width)
                total = total - mm_split(e_hi[:, ends], e_lo[:, ends], a_all[k])
            y_keep[...] = total
        y_low[...] = y_keep[...].astype(BF16)
        mapped_whole.wait_recv()

        def shared(i, start, size):
            return pl.ds(pl.multiple_of(ahead(i) * share + start, 16), size)

        def separator_rows(blocks):
            places = [shared(*block) for block in blocks]
            values = [mm(spread[place, :], y_low[...]) for place in places]
            return [value + mapped_rcv[place, :] for place, value in zip(places, values)]

        sent_out(0, 1, width)
        sends_c = scatter(separator_rows, share, s_rcv)
        get_r.wait()
        get_rr.wait()
        r_hi[...], r_lo[...] = halves(r_raw[...])
        for first in range(0, separator, step):
            ends = slice(first, first + step)
            rt_hi[ends, :], rt_lo[ends, :] = halves(r_raw[:, ends].T)
        sends_z = []
        for piece, (at, slot, fine) in enumerate(sends_c):
            total = gathered(s_rcv, at, slot, fine)
            part_own[at, :] = total
            z_snd[at, :] = total.astype(BF16)
            for d in range(1, subs):
                copy = pltpu.make_async_remote_copy(
                    z_snd.at[at],
                    z_rcv.at[d, at],
                    z_ssem.at[0],
                    z_rsem.at[piece],
                    device_id={"sub": lax.rem(sub + d, subs)},
                )
                copy.start()
            sends_z.append(at)
        turn_inverse()
        sent_out(1, 1, width)
        def root_block(i):
            ends = part(behind(i), share)
            right = rhs_hi[ends, :]
            return mm_split(r_hi[:, ends], r_lo[:, ends], right)

        fine = share // len(sends_z)
        for piece, at in enumerate(sends_z):
            block = z_rcv.at[pl.ds(1, subs - 1), at]
            pltpu.make_async_remote_copy(
                block, block, z_ssem.at[0], z_rsem.at[piece], device_id={"row": 1 - row}
            ).wait_recv()
            total = part_own[at, :]
            for d in range(1, subs):
                total = total + z_rcv[d, at, :].astype(F32)
            high, low = halves(root_right[at, :] - total)
            place = pl.ds(pl.multiple_of(col * share + piece * fine, 16), fine)
            rhs_hi[place, :] = high
            rhs_lo[place, :] = low
            share_out(rhs_hi.at[place])
        if whole_lanes:
            own = part(col, share)
            part_own[0:share, :] = mm(r_hi[:, own], rhs_lo[own, :]) + root_block(0)
            near_arrived(cols - 2, share)
            near_total = part_own[0:share, :]
            for i in range(2, cols):
                near_total = near_total + root_block(i)
            part_own[0:share, :] = near_total
            far_arrived(share)
            root_half = part_own[0:share, :] + root_block(1)
        else:
            part_own[0:share, :] = mm(r_hi[...], rhs_lo[...])
            near_arrived(cols - 2, share)
            far_arrived(share)
            root_half = mm_split(r_hi[...], r_lo[...], rhs_hi[...])
            root_half = root_half + part_own[0:share, :]
        w_pair[0:share, :] = paired(root_half)

        def coupled_block(i):
            ends = part(behind(i), share)
            return mm(spread_turn[:, ends], sep_low[ends, :])

        def root_rows(blocks):
            places = [shared(*block) for block in blocks]
            pair = w_pair[0:share, :]
            return [mm_paired(rt_hi[place, :], rt_lo[place, :], pair) for place in places]

        sent_out(0, 1, share)
        sends_e = scatter(root_rows, share, t_rcv)
        sent_out(1, 1, share)
        for piece, (at, slot, fine) in enumerate(sends_e):
            total = gathered(t_rcv, at, slot, fine)
            place = pl.ds(pl.multiple_of(col * share + piece * fine, 16), fine)
            sep_low[place, :] = total.astype(BF16)
            share_out(sep_low.at[place])
            root_out[at, :] = total
            root_keep[at, :] = total
        root_whole.start()
        if whole_lanes:
            y_keep[...] = y_keep[...] - coupled_block(0)
            near_arrived(cols - 2, share)
            total = y_keep[...]
            for i in range(2, cols):
                total = total - coupled_block(i)
            y_keep[...] = total
            far_arrived(share)
            sep_whole.start()
            w_pair[0:width, :] = paired(y_keep[...] - coupled_block(1))
        else:
            near_arrived(cols - 2, share)
            far_arrived(share)
            sep_whole.start()
            w_pair[0:width, :] = paired(y_keep[...] - mm(spread_turn[...], sep_low[...]))
        sent_out(0, 1, share)
        sends_g = scatter(turned, width, back_rcv)
        sent_out(1, 1, share)
        for at, slot, fine in sends_g:
            total = gathered(back_rcv, at, slot, fine)
            y_low[at, :] = total.astype(BF16)
            for i in list(range(1, cols)) + [0]:
                to_other(y_low.at[at], x_all.at[i, at], i).start()
            x_out[0, at, :] = total
        sent_across()
        sent_out(0, 1, width)
        sent_out(1, 0, width)
        finish([m_whole, root_whole, sep_whole])


def publish(x, root, x_out, root_out, sem):
    copies = [
        pltpu.make_async_copy(x, x_out, sem.at[0]),
        pltpu.make_async_copy(root, root_out, sem.at[1]),
    ]
    for copy in copies:
        copy.start()
    for copy in copies:
        copy.wait()


def shards(
    sizes,
    factor_cols,
    block_pattern,
    diag_inverse,
    coupling_cols,
    separator_rows,
    root_inverse,
    right_side,
    root_right,
):
    subs, cols = sizes
    width, panel = diag_inverse.shape[1:]
    share, separator = root_inverse.shape
    sources = right_side.shape[2]
    coupled = coupling_cols.shape[3]
    hbm = pl.BlockSpec(memory_space=pltpu.HBM)
    vmem = pl.BlockSpec(memory_space=pltpu.VMEM)
    V = pltpu.VMEM
    DMA = pltpu.SemaphoreType.DMA
    tile = (cols, width, width)
    most = max(width, share)
    scratch = [
        V((width, panel), F32),
        V((width, panel), BF16),
        V((width, coupled), BF16),
        V((share, separator), F32),
        V((panel, sources), F32),
        V((panel, 2 * sources), BF16),
        V((most, 2 * sources), BF16),
        V((width, panel), BF16),
        V((width, panel), BF16),
        V(tile, BF16),
        V(tile, BF16),
        V(tile, BF16),
        V((separator, width), BF16),
        V((width, separator), BF16),
        V((share, separator), BF16),
        V((share, separator), BF16),
        V((separator, share), BF16),
        V((separator, share), BF16),
        V((width, sources), F32),
        V((width, sources), BF16),
        V((separator, sources), F32),
        V((separator, sources), F32),
        V((most, sources), F32),
        V((cols, most, sources), BF16),
        V((cols, width, sources), BF16),
        V((cols, width, sources), BF16),
        V((cols, share, sources), BF16),
        V((share, sources), BF16),
        V((subs, share, sources), BF16),
        V((separator, sources), BF16),
        V((separator, sources), BF16),
        V((cols, share, sources), BF16),
        V((separator, sources), BF16),
        V((share, sources), F32),
        V((cols, width, sources), BF16),
        V((cols, width, sources), BF16),
        pltpu.SMEM(block_pattern.shape, jnp.int32),
        V(separator_rows.shape, jnp.int32),
        V(root_right.shape, F32),
        DMA((7 + CHUNKS,)),
        DMA((4 + CHUNKS,)),
        DMA((4 + CHUNKS,)),
        DMA((2,)),
        DMA((SLOTS + 3,)),
        DMA((1,)),
        DMA((SLOTS,)),
    ]
    inputs = (
        factor_cols,
        block_pattern,
        diag_inverse,
        coupling_cols,
        separator_rows,
        root_inverse,
        right_side,
        root_right,
    )
    shapes = (
        jax.ShapeDtypeStruct((1, width, sources), F32),
        jax.ShapeDtypeStruct((share, sources), F32),
    )
    x, root = pl.pallas_call(
        functools.partial(kernel, sizes),
        out_shape=shapes,
        in_specs=[hbm] * 8,
        out_specs=(vmem, vmem),
        scratch_shapes=scratch,
        compiler_params=pltpu.CompilerParams(
            collective_id=0, has_side_effects=True, vmem_limit_bytes=52 * 1024 * 1024
        ),
        name="tree_solve",
    )(*[pltpu.with_memory_space_constraint(value, pltpu.HBM) for value in inputs])
    return pl.pallas_call(
        publish,
        out_shape=shapes,
        in_specs=[vmem, vmem],
        out_specs=(hbm, hbm),
        scratch_shapes=[DMA((2,))],
        compiler_params=pltpu.CompilerParams(vmem_limit_bytes=2 * 1024 * 1024),
        name="publish",
    )(x, root)


def solution(mesh):
    sizes = (mesh.shape["sub"], mesh.shape["col"])
    return jax.shard_map(
        functools.partial(shards, sizes),
        mesh=mesh,
        in_specs=(
            P("sub", None, "col", "row"),
            P("sub", None, None),
            P("sub", ("row", "col"), None),
            P("sub", "row", "col", None),
            P("sub", None),
            P("col", None),
            P("sub", "row", None),
            P("col", None),
        ),
        out_specs=(P("sub", ("row", "col"), None), P("col", None)),
        check_vma=False,
    )
```

```python
import functools

import jax
import jax.numpy as jnp
from jax import lax
from jax.experimental import pallas as pl
from jax.experimental.pallas import tpu as pltpu
from jax.sharding import PartitionSpec as P

BLOCK = 256
F32 = jnp.float32
BF16 = jnp.bfloat16
CHUNKS = 2
BLOCKS = 4
SLOTS = 8


def mm(a, b):
    return lax.dot_general(a, b, (((1,), (0,)), ((), ())), preferred_element_type=F32)


def mm_nt(a, b):
    return lax.dot_general(a, b, (((1,), (1,)), ((), ())), preferred_element_type=F32)


def halves(x):
    high = x.astype(BF16)
    low = (x - high.astype(F32)).astype(BF16)
    return high, low


def paired(x):
    return jnp.concatenate(halves(x), axis=1)


def stacked(blocks, right):
    tall = mm(jnp.concatenate(blocks, axis=0), right) if len(blocks) > 1 else mm(blocks[0], right)
    values, at = [], 0
    for block in blocks:
        values.append(tall[at : at + block.shape[0], :])
        at += block.shape[0]
    return values


def mm_split(high, low, right):
    first, second = stacked([high, low], right)
    return first + second


def folded(both):
    sources = both.shape[1] // 2
    return both[:, :sources] + both[:, sources:]


def mm_paired(high, low, pair):
    return folded(mm_split(high, low, pair))


def mm_apart(high, low, pair):
    return folded(mm(high, pair) + mm(low, pair))


def divided(size, most):
    count = most
    while count > 1 and size % (16 * count):
        count //= 2
    return count


def offsets(cols):
    tall = max(s for s in range(1, cols + 1) if s * s <= cols and cols % s == 0)
    wide = cols // tall
    steps = [(y, x) for y in range(tall) for x in range(wide)]

    def hops(step):
        return min(step[0], tall - step[0]) + min(step[1], wide - step[1])

    far = sorted(steps[1:], key=lambda step: (-hops(step), -step[0], -step[1]))
    return tall, wide, [(0, 0)] + far


def kernel(
    sizes,
    factor_hbm,
    pattern_hbm,
    inverse_hbm,
    couple_hbm,
    rows_hbm,
    root_hbm,
    right_hbm,
    root_right_hbm,
    x_out,
    root_out,
    e_raw,
    m_raw,
    c_raw,
    r_raw,
    b_raw,
    b_pair,
    w_pair,
    e_hi,
    e_lo,
    et_hi,
    et_lo,
    m_turn,
    spread,
    spread_turn,
    r_hi,
    r_lo,
    rt_hi,
    rt_lo,
    y_keep,
    y_low,
    mapped_snd,
    mapped_rcv,
    part_own,
    part_snd,
    a_rcv,
    a_all,
    s_rcv,
    z_snd,
    z_rcv,
    rhs_hi,
    rhs_lo,
    t_rcv,
    sep_low,
    root_keep,
    back_rcv,
    x_all,
    pattern,
    rows_ref,
    root_right,
    load_sem,
    pair_snd,
    pair_rcv,
    col_snd,
    col_rcv,
    z_ssem,
    z_rsem,
):
    subs, cols = sizes
    sub = lax.axis_index("sub")
    row = lax.axis_index("row")
    col = lax.axis_index("col")
    width = e_raw.shape[0]
    panel = e_raw.shape[1]
    share = r_raw.shape[0]
    separator = r_raw.shape[1]
    tall, wide, steps = offsets(cols)
    whole_lanes = share % 128 == 0
    col_y = lax.div(col, wide)
    col_x = lax.rem(col, wide)

    def ahead(i):
        y, x = steps[i]
        return lax.rem(col_y + y, tall) * wide + lax.rem(col_x + x, wide)

    def behind(i):
        y, x = steps[i]
        return lax.rem(col_y + (tall - y), tall) * wide + lax.rem(col_x + (wide - x), wide)

    def load(source, target, index):
        return pltpu.make_async_copy(source, target, load_sem.at[index])

    thick = width // CHUNKS
    get_b = load(right_hbm.at[0], b_raw, 0)
    get_m = load(factor_hbm.at[0, 0], m_raw, 1)
    get_c = load(couple_hbm.at[0, 0], c_raw, 2)
    get_r = load(root_hbm, r_raw, 3)
    get_p = load(pattern_hbm, pattern, 4)
    get_n = load(rows_hbm, rows_ref, 5)
    get_rr = load(root_right_hbm, root_right, 6)
    get_e = []
    for c in range(CHUNKS):
        rows = pl.ds(c * thick, thick)
        get_e.append(load(inverse_hbm.at[0, rows], e_raw.at[rows], 7 + c))

    @pl.when(row == 0)
    def _():
        for copy in [get_b] + get_e + [get_n, get_c]:
            copy.start()

    @pl.when(row != 0)
    def _():
        for copy in [get_p, get_m, get_n, get_c]:
            copy.start()

    barrier = pltpu.get_barrier_semaphore()
    pl.semaphore_signal(barrier, inc=1, device_id={"row": 1 - row})
    for i in range(1, cols):
        pl.semaphore_signal(barrier, inc=1, device_id={"col": ahead(i)})
        pl.semaphore_signal(barrier, inc=1, device_id={"row": 1 - row, "col": ahead(i)})
    for d in range(1, subs):
        pl.semaphore_signal(barrier, inc=1, device_id={"sub": lax.rem(sub + d, subs)})

    def greet():
        pl.semaphore_wait(barrier, 1 + 2 * (cols - 1) + (subs - 1))

    def part(k, size):
        return pl.ds(pl.multiple_of(k * size, size), size)

    def to_pair(source, target, index):
        return pltpu.make_async_remote_copy(
            source, target, pair_snd.at[index], pair_rcv.at[index], device_id={"row": 1 - row}
        )

    def to_col(source, target, kind, slot, i):
        return pltpu.make_async_remote_copy(
            source, target, col_snd.at[kind], col_rcv.at[slot], device_id={"col": ahead(i)}
        )

    def gather_slot(i):
        return SLOTS + (2 if i == 0 else 0 if i == 1 else 1)

    def to_other(source, target, i):
        return pltpu.make_async_remote_copy(
            source,
            target,
            col_snd.at[1],
            col_rcv.at[gather_slot(i)],
            device_id={"row": 1 - row, "col": ahead(i)},
        )

    def arrived(slot, first, count, start, size):
        block = part_snd.at[pl.ds(first, count), pl.ds(start, size)]
        pltpu.make_async_remote_copy(
            block, block, col_snd.at[0], col_rcv.at[slot], device_id={"row": 1 - row}
        ).wait_recv()

    def far_arrived(size):
        arrived(SLOTS, 1, 1, 0, size)

    def near_arrived(count, size):
        arrived(SLOTS + 1, 0, count, 0, size)

    def scatter(make, size, receive):
        blocks = divided(size, BLOCKS)
        pieces = divided(size, SLOTS)
        tallest = size // blocks
        fine = size // pieces
        each = pieces // blocks
        batches = [[(1, 0)]]
        for block in range(blocks):
            batch = [(i, block) for i in range(2, cols)] + [(0, block)]
            if block + 1 < blocks:
                batch.insert(0, (1, block + 1))
            batches.append(batch)
        for batch in batches:
            values = make([(i, block * tallest, tallest) for i, block in batch])
            for (i, block), value in zip(batch, values):
                rows = pl.ds(block * tallest, tallest)
                if i > 0:
                    part_snd[i, rows, :] = value.astype(BF16)
                else:
                    part_own[rows, :] = value
            for turn in range(each):
                for i, block in batch:
                    if i > 0:
                        piece = block * each + turn
                        at = pl.ds(piece * fine, fine)
                        to_col(part_snd.at[i, at], receive.at[i, at], 0, piece, i).start()
        return [(pl.ds(piece * fine, fine), piece, fine) for piece in range(pieces)]

    def gathered(receive, at, slot, fine):
        arrived(slot, 1, cols - 1, 0, fine)
        total = part_own[at, :]
        for i in range(1, cols):
            total = total + receive[i, at, :].astype(F32)
        return total

    def share_out(target):
        for i in range(1, cols):
            to_col(target, target, 1, gather_slot(i), i).start()

    def sent_out(kind, first, size):
        block = part_snd.at[pl.ds(first, cols - first), pl.ds(0, size)]
        pltpu.make_async_remote_copy(
            block, block, col_snd.at[kind], col_rcv.at[0], device_id={"row": 1 - row}
        ).wait_send()

    def sent_across():
        block = z_rcv.at[pl.ds(1, subs - 1)]
        pltpu.make_async_remote_copy(
            block, block, z_ssem.at[0], z_rsem.at[0], device_id={"row": 1 - row}
        ).wait_send()

    def finish(copies):
        for copy in copies:
            copy.wait_send()

    def apply_inverse(c, put):
        rows = pl.ds(c * thick, thick)
        high, low = halves(e_raw[rows, :])
        e_hi[rows, :] = high
        e_lo[rows, :] = low
        put(rows, mm_paired(high, low, b_pair[...]))

    def turn_inverse():
        for i in range(cols):
            block = e_raw[:, part(ahead(i), width)]
            et_hi[i], et_lo[i] = halves(block.T)

    step = min(BLOCK, separator)

    def hits(first):
        at = lax.broadcasted_iota(jnp.int32, (step, rows_ref.shape[1]), 0) + first
        return jnp.where(at == rows_ref[...], 1.0, 0.0).astype(BF16)

    def make_spread():
        for first in range(0, separator, step):
            spread[first : first + step, :] = mm_nt(hits(first), c_raw[...]).astype(BF16)

    def make_spread_turn():
        for first in range(0, separator, step):
            spread_turn[:, first : first + step] = mm_nt(c_raw[...], hits(first)).astype(BF16)

    def turned(blocks):
        values = []
        for i, start, size in blocks:
            rows = pl.ds(start, size)
            values.append(mm_paired(et_hi[i, rows, :], et_lo[i, rows, :], w_pair[0:width, :]))
        return values

    y_parts = []
    for c in range(CHUNKS):
        rows = pl.ds(c * thick, thick)
        y_parts.append(to_pair(y_low.at[rows], y_low.at[rows], 4 + c))
    m_whole = to_pair(m_raw, m_raw, 0)
    mapped_whole = to_pair(mapped_snd, mapped_rcv, 1)
    sep_whole = to_pair(sep_low, sep_low, 2)
    root_whole = to_pair(root_keep, root_keep, 3)

    @pl.when(row == 0)
    def _():
        def put(rows, value):
            y_keep[rows, :] = value
            y_low[rows, :] = value.astype(BF16)

        get_b.wait()
        b_pair[...] = paired(b_raw[...])
        for copy in get_e:
            copy.wait()
        for c in range(CHUNKS):
            apply_inverse(c, put)
        greet()
        for copy in y_parts:
            copy.start()
        get_c.wait()
        get_n.wait()
        make_spread()
        mapped_snd[...] = mm(spread[...], y_low[...])
        mapped_whole.start()
        make_spread_turn()
        turn_inverse()
        sep_whole.wait_recv()
        y_keep[...] = y_keep[...] - mm(spread_turn[...], sep_low[...])
        root_whole.wait_recv()
        root_out[...] = root_keep[...]
        m_whole.wait_recv()
        near = list(range(2, cols))
        for group in ([0], near, [1]):
            if group is near:
                near_arrived(cols - 2, width)
            elif group[0] > 0:
                far_arrived(width)
            else:
                arrived(SLOTS + 2, 0, 1, 0, width)
            total = y_keep[...]
            for i in group:
                total = total - mm(m_raw[:, part(behind(i), width)], x_all[i])
            if group[0] != 1:
                y_keep[...] = total
            else:
                w_pair[0:width, :] = paired(total)
        sends = scatter(turned, width, back_rcv)
        for at, slot, fine in sends:
            x_out[0, at, :] = gathered(back_rcv, at, slot, fine)
        sent_out(0, 1, width)
        finish(y_parts + [mapped_whole])

    @pl.when(row != 0)
    def _():
        high_rows = min(width, BLOCK)
        get_p.wait()
        get_m.wait()
        for at in range(0, width, high_rows):
            column = lax.div(col * width + at, BLOCK)
            for block in range(panel // BLOCK):
                present = pattern[0, panel // BLOCK + block, column].astype(F32)
                ends = slice(block * BLOCK, (block + 1) * BLOCK)
                kept = m_raw[at : at + high_rows, ends].astype(F32) * present
                m_raw[at : at + high_rows, ends] = kept.astype(BF16)
        greet()
        for copy in [get_b] + get_e + [get_r, get_rr]:
            copy.start()
        m_whole.start()
        for i in range(cols):
            block = m_raw[:, part(ahead(i), width)]
            m_turn[i] = block.astype(F32).T.astype(BF16)
        rhs_lo[...] = jnp.zeros(rhs_lo.shape, BF16)
        get_c.wait()
        get_n.wait()
        make_spread()
        for copy in y_parts:
            copy.wait_recv()

        def a_rows(blocks):
            rows = [m_turn[i, pl.ds(start, size), :] for i, start, size in blocks]
            return [mm(block, y_low[...]) for block in rows]

        sends_a = scatter(a_rows, width, a_rcv)

        def put(rows, value):
            y_keep[rows, :] = value

        get_b.wait()
        b_pair[...] = paired(b_raw[...])
        for copy in get_e:
            copy.wait()
        apply_inverse(0, put)
        for at, slot, fine in sends_a:
            a_all[col, at, :] = gathered(a_rcv, at, slot, fine).astype(BF16)
            share_out(a_all.at[col, at])
        for c in range(1, CHUNKS):
            apply_inverse(c, put)
        near = list(range(2, cols))
        for group in ([0], near, [1]):
            if group is near:
                near_arrived(cols - 2, width)
            elif group[0] > 0:
                far_arrived(width)
            total = y_keep[...]
            for i in group:
                k = behind(i)
                ends = part(k, width)
                total = total - mm_split(e_hi[:, ends], e_lo[:, ends], a_all[k])
            y_keep[...] = total
        y_low[...] = y_keep[...].astype(BF16)
        mapped_whole.wait_recv()

        def shared(i, start, size):
            return pl.ds(pl.multiple_of(ahead(i) * share + start, 16), size)

        def separator_rows(blocks):
            places = [shared(*block) for block in blocks]
            values = [mm(spread[place, :], y_low[...]) for place in places]
            return [value + mapped_rcv[place, :] for place, value in zip(places, values)]

        sent_out(0, 1, width)
        sends_c = scatter(separator_rows, share, s_rcv)
        get_r.wait()
        get_rr.wait()
        r_hi[...], r_lo[...] = halves(r_raw[...])
        for first in range(0, separator, step):
            ends = slice(first, first + step)
            rt_hi[ends, :], rt_lo[ends, :] = halves(r_raw[:, ends].T)
        sends_z = []
        for piece, (at, slot, fine) in enumerate(sends_c):
            total = gathered(s_rcv, at, slot, fine)
            part_own[at, :] = total
            z_snd[at, :] = total.astype(BF16)
            for d in sorted(range(1, subs), key=lambda d: -min(d, subs - d)):
                copy = pltpu.make_async_remote_copy(
                    z_snd.at[at],
                    z_rcv.at[d, at],
                    z_ssem.at[0],
                    z_rsem.at[piece],
                    device_id={"sub": lax.rem(sub + d, subs)},
                )
                copy.start()
            sends_z.append(at)
        make_spread_turn()
        sent_out(1, 1, width)
        def root_block(i):
            ends = part(behind(i), share)
            right = rhs_hi[ends, :]
            return mm_split(r_hi[:, ends], r_lo[:, ends], right)

        fine = share // len(sends_z)
        for piece, at in enumerate(sends_z):
            block = z_rcv.at[pl.ds(1, subs - 1), at]
            pltpu.make_async_remote_copy(
                block, block, z_ssem.at[0], z_rsem.at[piece], device_id={"row": 1 - row}
            ).wait_recv()
            total = part_own[at, :]
            for d in range(1, subs):
                total = total + z_rcv[d, at, :].astype(F32)
            high, low = halves(root_right[at, :] - total)
            place = pl.ds(pl.multiple_of(col * share + piece * fine, 16), fine)
            rhs_hi[place, :] = high
            rhs_lo[place, :] = low
            share_out(rhs_hi.at[place])
        if whole_lanes:
            own = part(col, share)
            part_own[0:share, :] = mm(r_hi[:, own], rhs_lo[own, :]) + root_block(0)
            turn_inverse()
            near_arrived(cols - 2, share)
            near_total = part_own[0:share, :]
            for i in range(2, cols):
                near_total = near_total + root_block(i)
            part_own[0:share, :] = near_total
            far_arrived(share)
            root_half = part_own[0:share, :] + root_block(1)
        else:
            part_own[0:share, :] = mm(r_hi[...], rhs_lo[...])
            turn_inverse()
            near_arrived(cols - 2, share)
            far_arrived(share)
            root_half = mm_split(r_hi[...], r_lo[...], rhs_hi[...])
            root_half = root_half + part_own[0:share, :]
        w_pair[0:share, :] = paired(root_half)

        def coupled_block(i):
            ends = part(behind(i), share)
            return mm(spread_turn[:, ends], sep_low[ends, :])

        def root_rows(blocks):
            places = [shared(*block) for block in blocks]
            pair = w_pair[0:share, :]
            return [mm_paired(rt_hi[place, :], rt_lo[place, :], pair) for place in places]

        sent_out(0, 1, share)
        sends_e = scatter(root_rows, share, t_rcv)
        sent_out(1, 1, share)
        for piece, (at, slot, fine) in enumerate(sends_e):
            total = gathered(t_rcv, at, slot, fine)
            place = pl.ds(pl.multiple_of(col * share + piece * fine, 16), fine)
            sep_low[place, :] = total.astype(BF16)
            share_out(sep_low.at[place])
            root_out[at, :] = total
            root_keep[at, :] = total
        root_whole.start()
        if whole_lanes:
            y_keep[...] = y_keep[...] - coupled_block(0)
            near_arrived(cols - 2, share)
            total = y_keep[...]
            for i in range(2, cols):
                total = total - coupled_block(i)
            y_keep[...] = total
            far_arrived(share)
            sep_whole.start()
            w_pair[0:width, :] = paired(y_keep[...] - coupled_block(1))
        else:
            near_arrived(cols - 2, share)
            far_arrived(share)
            sep_whole.start()
            w_pair[0:width, :] = paired(y_keep[...] - mm(spread_turn[...], sep_low[...]))
        sent_out(0, 1, share)
        sends_g = scatter(turned, width, back_rcv)
        sent_out(1, 1, share)
        for at, slot, fine in sends_g:
            total = gathered(back_rcv, at, slot, fine)
            y_low[at, :] = total.astype(BF16)
            for i in list(range(1, cols)) + [0]:
                to_other(y_low.at[at], x_all.at[i, at], i).start()
            x_out[0, at, :] = total
        sent_across()
        sent_out(0, 1, width)
        sent_out(1, 0, width)
        finish([m_whole, root_whole, sep_whole])


def publish(x, root, x_out, root_out, sem):
    copies = [
        pltpu.make_async_copy(x, x_out, sem.at[0]),
        pltpu.make_async_copy(root, root_out, sem.at[1]),
    ]
    for copy in copies:
        copy.start()
    for copy in copies:
        copy.wait()


def shards(
    sizes,
    factor_cols,
    block_pattern,
    diag_inverse,
    coupling_cols,
    separator_rows,
    root_inverse,
    right_side,
    root_right,
):
    subs, cols = sizes
    width, panel = diag_inverse.shape[1:]
    share, separator = root_inverse.shape
    sources = right_side.shape[2]
    coupled = coupling_cols.shape[3]
    hbm = pl.BlockSpec(memory_space=pltpu.HBM)
    vmem = pl.BlockSpec(memory_space=pltpu.VMEM)
    V = pltpu.VMEM
    DMA = pltpu.SemaphoreType.DMA
    tile = (cols, width, width)
    most = max(width, share)
    scratch = [
        V((width, panel), F32),
        V((width, panel), BF16),
        V((width, coupled), BF16),
        V((share, separator), F32),
        V((panel, sources), F32),
        V((panel, 2 * sources), BF16),
        V((most, 2 * sources), BF16),
        V((width, panel), BF16),
        V((width, panel), BF16),
        V(tile, BF16),
        V(tile, BF16),
        V(tile, BF16),
        V((separator, width), BF16),
        V((width, separator), BF16),
        V((share, separator), BF16),
        V((share, separator), BF16),
        V((separator, share), BF16),
        V((separator, share), BF16),
        V((width, sources), F32),
        V((width, sources), BF16),
        V((separator, sources), F32),
        V((separator, sources), F32),
        V((most, sources), F32),
        V((cols, most, sources), BF16),
        V((cols, width, sources), BF16),
        V((cols, width, sources), BF16),
        V((cols, share, sources), BF16),
        V((share, sources), BF16),
        V((subs, share, sources), BF16),
        V((separator, sources), BF16),
        V((separator, sources), BF16),
        V((cols, share, sources), BF16),
        V((separator, sources), BF16),
        V((share, sources), F32),
        V((cols, width, sources), BF16),
        V((cols, width, sources), BF16),
        pltpu.SMEM(block_pattern.shape, jnp.int32),
        V(separator_rows.shape, jnp.int32),
        V(root_right.shape, F32),
        DMA((7 + CHUNKS,)),
        DMA((4 + CHUNKS,)),
        DMA((4 + CHUNKS,)),
        DMA((2,)),
        DMA((SLOTS + 3,)),
        DMA((1,)),
        DMA((SLOTS,)),
    ]
    inputs = (
        factor_cols,
        block_pattern,
        diag_inverse,
        coupling_cols,
        separator_rows,
        root_inverse,
        right_side,
        root_right,
    )
    shapes = (
        jax.ShapeDtypeStruct((1, width, sources), F32),
        jax.ShapeDtypeStruct((share, sources), F32),
    )
    x, root = pl.pallas_call(
        functools.partial(kernel, sizes),
        out_shape=shapes,
        in_specs=[hbm] * 8,
        out_specs=(vmem, vmem),
        scratch_shapes=scratch,
        compiler_params=pltpu.CompilerParams(
            collective_id=0, has_side_effects=True, vmem_limit_bytes=52 * 1024 * 1024
        ),
        name="tree_solve",
    )(*[pltpu.with_memory_space_constraint(value, pltpu.HBM) for value in inputs])
    return pl.pallas_call(
        publish,
        out_shape=shapes,
        in_specs=[vmem, vmem],
        out_specs=(hbm, hbm),
        scratch_shapes=[DMA((2,))],
        compiler_params=pltpu.CompilerParams(vmem_limit_bytes=2 * 1024 * 1024),
        name="publish",
    )(x, root)


def solution(mesh):
    sizes = (mesh.shape["sub"], mesh.shape["col"])
    return jax.shard_map(
        functools.partial(shards, sizes),
        mesh=mesh,
        in_specs=(
            P("sub", None, "col", "row"),
            P("sub", None, None),
            P("sub", ("row", "col"), None),
            P("sub", "row", "col", None),
            P("sub", None),
            P("col", None),
            P("sub", "row", None),
            P("col", None),
        ),
        out_specs=(P("sub", ("row", "col"), None), P("col", None)),
        check_vma=False,
    )
```
